32 devices in a mesh: wave: 8 (over z, y), lev: 4 (over x, core).
Axes of the slice: x: 2, y: 2, z: 4, core: 2. Of those that a mesh axis runs over, the one named last changes fastest.
Arguments:
- spectral: float32 [8, 136, 2, 1280], P('wave', 'lev'), may hold values from -6 to 6
- to_modes: float32 [136, 136], replicated
- from_modes: float32 [136, 136], replicated
- mode_depths: float32 [136], replicated, may hold values from 0.05 to 5
- legendre: float32 [8, 16, 1280], P('wave'), may hold values from -0.03125 to 0.03125
- wave_ids: int32 [8], replicated, may hold values from 0 to 1279, as said below
- lat_points: int32 [16], P('wave'), may hold values from 20 to 5136, as said below
Outputs:
- grid: float32 [136, 16, 5136], P('lev', 'wave')
The draws below stay inside these ranges and needn't reach their ends.
Inputs may be any that keep to these rules, and one draw needn't show every extreme that they name: `wave_ids`: distinct and ascending; 0 and 1279 are always among them. `lat_points`: each is 20 + 4 k for a whole k; not falling along the latitudes; the last is always 5136.
All inputs are finite; a program needn't handle non-finite values.
Results may differ from the reference program's by a relative error of at most 0.0003.
Values sent between devices are 32-bit elements; how exact they have to be, the bound alone decides.
No kernel may reach another device: no remote copies, remote signals or barrier semaphores. Data moves between devices by JAX's collectives and lax.ppermute only.
A program may use at most 64 MiB of HBM per device.

```python
import math
import jax
import jax.numpy as jnp
from jax import lax

LEV = 136
NT = 1280
LONS = 5136
WAVES = 8
LATS = 16


def mode_matrix(key):
    eye_part = jnp.eye(LEV, dtype=jnp.float32)
    spread = jax.random.normal(key, (LEV, LEV), jnp.float32) * 0.5
    return eye_part + spread / math.sqrt(LEV)


def draw_to_modes(key, part):
    return mode_matrix(jax.random.fold_in(key, 11))


def draw_from_modes(key, part):
    return mode_matrix(jax.random.fold_in(key, 12))


def draw_wave_ids(key, part):
    shuffled = jax.random.permutation(jax.random.fold_in(key, 13), NT - 2) + 1
    picked = shuffled[:WAVES - 2]
    joined = jnp.concatenate([jnp.zeros((1,), jnp.int32), picked.astype(jnp.int32), jnp.full((1,), NT - 1, jnp.int32)])
    return jnp.sort(joined).astype(jnp.int32)


def draw_lat_points(key, part):
    top_index = (LONS - 20) // 4
    steps_drawn = jax.random.randint(jax.random.fold_in(key, 14), (LATS,), 0, top_index + 1)
    steps_drawn = jnp.sort(steps_drawn).at[LATS - 1].set(top_index)
    return (20 + 4 * steps_drawn).astype(jnp.int32)


def block_scale(stream_key, dims, split, least, largest):
    gain, own = 1.0, jax.random.fold_in(stream_key, 6)
    for dim, shards_of in split:
        draws = jnp.exp(jax.random.uniform(jax.random.fold_in(own, dim), (shards_of,), jnp.float32, least / len(split), largest / len(split)))
        gain = gain * jnp.repeat(draws, dims[dim] // shards_of).reshape([-1 if axis == dim else 1 for axis in range(len(dims))])
    return gain


def noise(own_key, shape, scale, limit, split=(), held_as=jnp.bfloat16):
    array = scale * jax.random.normal(own_key, shape, jnp.float32)
    if split:
        array = array * block_scale(own_key, shape, split, -0.22, 0.18)
    return jnp.clip(array, -limit, limit).astype(held_as)


def setup_inputs(seed: int = 0) -> dict:
    arg_keys = jax.random.split(jax.random.key(seed), 8)
    spectral = noise(arg_keys[0], (WAVES, LEV, 2, NT), 1.0, 6.0, ((0, 8), (1, 4)), jnp.float32)
    to_modes = draw_to_modes(jax.random.fold_in(arg_keys[7], 71), 0)
    from_modes = draw_from_modes(jax.random.fold_in(arg_keys[7], 71), 0)
    mode_depths = jnp.clip(jnp.exp(jax.random.uniform(arg_keys[3], (LEV,), jnp.float32, math.log(0.05), math.log(5.0))), 0.05, 5.0)
    legendre = noise(arg_keys[4], (WAVES, LATS, NT), (NT * WAVES * 4) ** -0.5, 0.03125, ((0, 8),), jnp.float32)
    wave_ids = draw_wave_ids(jax.random.fold_in(arg_keys[7], 71), 0)
    lat_points = draw_lat_points(jax.random.fold_in(arg_keys[7], 71), 0)
    return {"spectral": spectral, "to_modes": to_modes, "from_modes": from_modes, "mode_depths": mode_depths, "legendre": legendre, "wave_ids": wave_ids, "lat_points": lat_points}


two_pi = 2.0 * math.pi


def reference(spectral, to_modes, from_modes, mode_depths, legendre, wave_ids, lat_points):
    highest = lax.Precision.HIGHEST
    mode_coeffs = jnp.einsum("kl,wlcn->wkcn", to_modes, spectral, precision=highest)
    orders = jnp.arange(NT).astype(jnp.float32)
    damping = 1.0 + mode_depths[:, None] * (orders * (orders + 1.0))[None, :] / float(NT * NT)
    divergence = jnp.einsum("lk,wkcn->wlcn", from_modes, mode_coeffs / damping[None, :, None, :], precision=highest)
    keep_mask = (jnp.arange(NT).astype(jnp.int32)[None, :] >= wave_ids[:, None]).astype(jnp.float32)
    masked = legendre * keep_mask[:, None, :]
    fourier = jnp.einsum("wjn,wlcn->lwcj", masked, divergence, precision=highest)
    positions = jnp.arange(LONS).astype(jnp.int32)

    def one_row(inputs):
        coeffs, points = inputs
        residue = (wave_ids[:, None] * positions[None, :]) % points
        phases = jnp.float32(two_pi) * residue.astype(jnp.float32) / points.astype(jnp.float32)
        weight = jnp.where(2 * wave_ids < points, jnp.where(wave_ids == 0, 1.0, 2.0), 0.0).astype(jnp.float32)
        basis_table = jnp.concatenate([jnp.cos(phases) * weight[:, None], jnp.sin(phases) * weight[:, None]], 0)
        coefficient = jnp.concatenate([coeffs[:, :, 0], -coeffs[:, :, 1]], 1)
        lat_row = jnp.dot(coefficient, basis_table, precision=highest)
        return lat_row * (positions < points).astype(jnp.float32)[None, :]

    lat_rows = lax.map(one_row, (jnp.moveaxis(fourier, 3, 0), lat_points))
    return jnp.transpose(lat_rows, (1, 0, 2))
```

```python
import functools
import math

import jax
import jax.numpy as jnp
from jax import lax
from jax.experimental import pallas as pl
from jax.experimental.pallas import tpu as pltpu
from jax.sharding import PartitionSpec as P

LONS = 5136
F32, BF16 = jnp.float32, jnp.bfloat16


def split(x):
    hi = x.astype(BF16)
    return hi, (x - hi.astype(F32)).astype(BF16)


def dot3(a, b, contract):
    dot = functools.partial(
        lax.dot_general, dimension_numbers=(contract, ((), ())), preferred_element_type=F32
    )
    return dot(a[0], b[0]) + (dot(a[0], b[1]) + dot(a[1], b[0]))


def send_kernel(lev_devices, waves, ids_ref, spec_ref, to_ref, from_ref, depth_ref, leg_ref, out_ref, cols_ref, tile_ref):
    levels = to_ref.shape[0]
    here = levels // lev_devices
    orders = leg_ref.shape[2]
    rows_here = leg_ref.shape[1] // waves
    lev, wave = lax.axis_index("lev"), lax.axis_index("wave")

    for d in range(lev_devices):

        @pl.when(lev == d)
        def _():
            cols_ref[...] = to_ref[:, d * here : (d + 1) * here]

    cols = split(cols_ref[...])
    eye = lax.broadcasted_iota(jnp.int32, (levels, levels), 0) == lax.broadcasted_iota(
        jnp.int32, (levels, levels), 1
    )
    depth = jnp.sum(jnp.where(eye, depth_ref[...][None, :], 0.0), axis=1, keepdims=True)
    n = lax.broadcasted_iota(jnp.int32, (1, orders), 1)
    nf = n.astype(F32)
    inverse = 1.0 / (1.0 + depth * (nf * (nf + 1.0) / float(orders * orders)))
    keep = n >= ids_ref[wave]
    tiles = orders // 128
    for t in range(tiles):
        tile_ref[t] = leg_ref[0, :, t * 128 : (t + 1) * 128]
    leg = jnp.concatenate(
        [
            jnp.concatenate([tile_ref[t, pl.ds(j, waves, stride=rows_here), :] for t in range(tiles)], 1)
            for j in range(rows_here)
        ],
        0,
    )
    leg = split(jnp.where(keep, leg, 0.0))
    back = split(from_ref[...])

    for c in range(2):
        spec = split(spec_ref[0, :, c, :])
        modes = dot3(cols, spec, ((1,), (0,))) * inverse
        sums = split(dot3(leg, split(modes), ((1,), (1,))))
        four = dot3(sums, back, ((1,), (1,)))
        for d in range(lev_devices):
            for j in range(rows_here):
                out_ref[d * waves : (d + 1) * waves, pl.ds((c * rows_here + j) * here, here)] = four[
                    j * waves : (j + 1) * waves, d * here : (d + 1) * here
                ]


def turn(m, i, p, inv_p):
    x = m * i
    r = x - jnp.floor(x * inv_p) * p
    r = jnp.where(r < 0.0, r + p, r)
    r = jnp.where(r >= p, r - p, r)
    quarter = jnp.floor(4.0 * r * inv_p + 0.5)
    v = (4.0 * r - quarter * p) * ((math.pi / 2) * inv_p)
    s = v * v
    sin = v + v * s * (-1.0 / 6 + s * (1.0 / 120 + s * (-1.0 / 5040 + s * (1.0 / 362880))))
    cos = 1.0 + s * (-0.5 + s * (1.0 / 24 + s * (-1.0 / 720 + s * (1.0 / 40320))))
    odd = (quarter == 1.0) | (quarter == 3.0)
    a, b = jnp.where(odd, sin, cos), jnp.where(odd, cos, sin)
    return (
        jnp.where((quarter == 1.0) | (quarter == 2.0), -a, a),
        jnp.where((quarter == 2.0) | (quarter == 3.0), -b, b),
    )


def grid_kernel(ids_ref, pts_ref, got_ref, out_ref, lhs_ref):
    here, rows_here, lons = out_ref.shape
    waves = ids_ref.shape[0]
    lev_devices = got_ref.shape[0] // waves
    pitch = -(-here // 8) * 8
    chunk = 1280
    starts = list(range(0, lons - chunk // 2, chunk))
    ends = starts[1:] + [lons]
    widest = -(-max(e - s for s, e in zip(starts, ends)) // 128) * 128

    total = got_ref[0:waves, :]
    for d in range(1, lev_devices):
        total = total + got_ref[d * waves : (d + 1) * waves, :]
    row = lax.broadcasted_iota(jnp.int32, (waves, 128), 0)
    m = jnp.zeros((waves, 128), F32)
    for w in range(waves):
        m = jnp.where(row == w, ids_ref[w].astype(F32), m)
    lhs_ref[...] = jnp.zeros_like(lhs_ref)
    lane = lax.broadcasted_iota(jnp.int32, (1, widest), 1).astype(F32)
    points, inner = [], []
    for j in range(rows_here):
        p = pts_ref[j].astype(F32)
        inv_p = 1.0 / jnp.full((1, 1), p, F32)
        mw = m[:, :here]
        weight = jnp.where(2.0 * mw < p, jnp.where(mw == 0.0, 1.0, 2.0), 0.0)
        for c in range(2):
            k, l = (j * 2 + c) * waves, (c * rows_here + j) * here
            part = total[:, l : l + here] * weight
            lhs_ref[k : k + waves, j * pitch : j * pitch + here] = -part if c else part
        points.append((p, inv_p))
        inner.append(turn(m[:, :1], lane, p, inv_p))
    hi, lo = split(lhs_ref[...])
    lhs = jnp.concatenate([hi, hi, lo], 0)
    for start, end in zip(starts, ends):
        size = end - start
        wide = -(-size // 128) * 128
        rows = []
        for j in range(rows_here):
            p, inv_p = points[j]
            ca, sa = turn(m[:, :1], float(start), p, inv_p)
            cb, sb = inner[j][0][:, :wide], inner[j][1][:, :wide]
            inside = lane[:, :wide] < p - float(start)
            rows += [
                jnp.where(inside, ca * cb - sa * sb, 0.0),
                jnp.where(inside, sa * cb + ca * sb, 0.0),
            ]
        hi, lo = split(jnp.concatenate(rows, 0))
        out = lax.dot_general(
            lhs,
            jnp.concatenate([hi, lo, hi], 0),
            (((0,), (0,)), ((), ())),
            preferred_element_type=F32,
        )
        for j in range(rows_here):
            out_ref[:, j, start:end] = out[j * pitch : j * pitch + here, :size]


def on_device(spectral, to_modes, from_modes, mode_depths, legendre, wave_ids, lat_points):
    lev_devices, waves = lax.axis_size("lev"), lax.axis_size("wave")
    here, rows_here = spectral.shape[1], lat_points.shape[0]
    smem = pl.BlockSpec(memory_space=pltpu.SMEM)
    vmem = pl.BlockSpec(memory_space=pltpu.VMEM)
    blocks = pl.pallas_call(
        functools.partial(send_kernel, lev_devices, waves),
        out_shape=jax.ShapeDtypeStruct((lev_devices * waves, 2 * rows_here * here), F32),
        in_specs=[smem] + [vmem] * 5,
        out_specs=vmem,
        scratch_shapes=[
            pltpu.VMEM((to_modes.shape[0], here), F32),
            pltpu.VMEM((legendre.shape[2] // 128, legendre.shape[1], 128), F32),
        ],
        name="send",
    )(wave_ids, spectral, to_modes, from_modes, mode_depths, legendre)
    got = lax.all_to_all(blocks, ("lev", "wave"), 0, 0, tiled=True)
    pitch = -(-here // 8) * 8
    return pl.pallas_call(
        grid_kernel,
        out_shape=jax.ShapeDtypeStruct((here, rows_here, LONS), F32),
        in_specs=[smem, smem, vmem],
        out_specs=vmem,
        scratch_shapes=[pltpu.VMEM((2 * rows_here * waves, rows_here * pitch), F32)],
        name="grid",
    )(wave_ids, lat_points, got)


def solution(mesh):
    return jax.shard_map(
        on_device,
        mesh=mesh,
        in_specs=(
            P("wave", "lev", None, None),
            P(),
            P(),
            P(),
            P("wave", None, None),
            P(),
            P("wave"),
        ),
        out_specs=P("lev", "wave", None),
        check_vma=False,
    )
```

```python
import functools
import math

import jax
import jax.numpy as jnp
from jax import lax
from jax.experimental import pallas as pl
from jax.experimental.pallas import tpu as pltpu
from jax.sharding import PartitionSpec as P

LONS = 5136
LANES = 128
CHUNK = 1280
F32, BF16 = jnp.float32, jnp.bfloat16


def up(size, to):
    return -(-size // to) * to


def split(x):
    hi = x.astype(BF16)
    return hi, (x - hi.astype(F32)).astype(BF16)


def dot(a, b, contract):
    return lax.dot_general(a, b, (contract, ((), ())), preferred_element_type=F32)


def send_kernel(
    lev_devices, waves,
    ids_hbm, to_hbm, depth_hbm, leg_hbm, from_hbm, spec_hbm,
    out_ref,
    ids_ref, to_ref, depth_ref, leg_ref, from_ref, spec_ref, cols_ref, tile_ref, back_ref, sems,
):
    copies = [
        pltpu.make_async_copy(source, target, sems.at[i])
        for i, (source, target) in enumerate(
            (
                (spec_hbm, spec_ref),
                (to_hbm, to_ref),
                (depth_hbm, depth_ref),
                (leg_hbm, leg_ref),
                (ids_hbm, ids_ref),
                (from_hbm, from_ref),
            )
        )
    ]
    for copy in copies:
        copy.start()
    levels = to_ref.shape[0]
    here = levels // lev_devices
    orders = leg_ref.shape[2]
    rows_here = leg_ref.shape[1] // waves
    parts = 2 * rows_here
    modes_up, here_up = up(levels, 16), up(here, 16)
    tiles = orders // LANES
    lev, wave = lax.axis_index("lev"), lax.axis_index("wave")
    cols_ref[...] = jnp.zeros_like(cols_ref)
    back_ref[...] = jnp.zeros_like(back_ref)
    tile_ref[...] = jnp.zeros_like(tile_ref)
    for copy in copies[1:]:
        copy.wait()

    for d in range(lev_devices):

        @pl.when(lev == d)
        def _():
            x = to_ref[:, d * here : (d + 1) * here]
            hi = x.astype(BF16).astype(F32)
            cols_ref[:levels, 0:here] = hi
            cols_ref[:levels, here_up : here_up + here] = hi
            cols_ref[:levels, 2 * here_up : 2 * here_up + here] = x - hi

    cols = cols_ref[...].astype(BF16)
    eye = lax.broadcasted_iota(jnp.int32, (levels, levels), 0) == lax.broadcasted_iota(
        jnp.int32, (levels, levels), 1
    )
    depth = jnp.sum(jnp.where(eye, depth_ref[...][None, :], 0.0), axis=1, keepdims=True)
    depth = jnp.concatenate([depth, jnp.zeros((modes_up - levels, 1), F32)], 0)
    n = lax.broadcasted_iota(jnp.int32, (1, orders), 1)
    nf = n.astype(F32)
    inverse = 1.0 / (1.0 + depth * (nf * (nf + 1.0) / float(orders * orders)))
    for t in range(tiles):
        tile_ref[2, t, : leg_ref.shape[1]] = leg_ref[0, :, t * LANES : (t + 1) * LANES]
        for j in range(rows_here):
            x = tile_ref[2, t, pl.ds(j, waves, stride=rows_here), :]
            for c in range(2):
                tile_ref[c, t, pl.ds(c * rows_here + j, waves, stride=parts), :] = x
    keep = n >= ids_ref[wave]
    leg = [
        split(jnp.where(keep, jnp.concatenate([tile_ref[c, t] for t in range(tiles)], 1), 0.0))
        for c in range(2)
    ]
    leg_hi = jnp.concatenate([leg[0][0], leg[1][0]], 1)
    leg_lo = jnp.concatenate([leg[0][1], leg[1][1]], 1)
    leg_both = jnp.concatenate([leg_hi, leg_lo], 0)
    back = from_ref[...].T
    for d in range(lev_devices):
        back_ref[:levels, d * LANES : d * LANES + here] = back[:, d * here : (d + 1) * here]
    back_hi, back_lo = split(back_ref[...])
    back = jnp.concatenate([back_hi, back_lo, back_hi], 0)
    copies[0].wait()

    modes = []
    for c in range(2):
        hi, lo = split(
            jnp.concatenate([spec_ref[0, :, c, :], jnp.zeros((here_up - here, orders), F32)], 0)
        )
        x = dot(cols, jnp.concatenate([hi, lo, hi], 0), ((1,), (0,)))
        modes.append(split(x * inverse))
    hi = jnp.concatenate([modes[0][0], modes[1][0]], 1)
    lo = jnp.concatenate([modes[0][1], modes[1][1]], 1)
    x = dot(hi, leg_both, ((1,), (1,)))
    y = dot(lo, leg_hi, ((1,), (1,)))
    width = parts * waves
    hi, lo = split(x[:, :width] + (x[:, width:] + y))
    four = dot(jnp.concatenate([hi, hi, lo], 0), back, ((0,), (0,)))
    for d in range(lev_devices):
        out_ref[d * width : (d + 1) * width, :] = four[:, d * LANES : (d + 1) * LANES]


def turn(m, i, p, inv_p):
    x = m * i
    r = x - jnp.floor(x * inv_p) * p
    r = jnp.where(r < 0.0, r + p, r)
    r = jnp.where(r >= p, r - p, r)
    quarter = jnp.floor(4.0 * r * inv_p + 0.5)
    v = (4.0 * r - quarter * p) * ((math.pi / 2) * inv_p)
    s = v * v
    sin = v + v * s * (-1.0 / 6 + s * (1.0 / 120 + s * (-1.0 / 5040 + s * (1.0 / 362880))))
    cos = 1.0 + s * (-0.5 + s * (1.0 / 24 + s * (-1.0 / 720 + s * (1.0 / 40320))))
    odd = (quarter == 1.0) | (quarter == 3.0)
    a, b = jnp.where(odd, sin, cos), jnp.where(odd, cos, sin)
    return (
        jnp.where((quarter == 1.0) | (quarter == 2.0), -a, a),
        jnp.where((quarter == 2.0) | (quarter == 3.0), -b, b),
    )


def chunks(lons):
    starts = list(range(0, lons - CHUNK // 2, CHUNK))
    return list(zip(starts, starts[1:] + [lons]))


def table_kernel(ids_hbm, pts_hbm, out_ref, ids_ref, pts_ref, sems):
    copies = [
        pltpu.make_async_copy(ids_hbm, ids_ref, sems.at[0]),
        pltpu.make_async_copy(pts_hbm, pts_ref, sems.at[1]),
    ]
    for copy in copies:
        copy.start()
    for copy in copies:
        copy.wait()
    rows_here = out_ref.shape[0]
    lons = out_ref.shape[3]
    waves = ids_ref.shape[0]
    widest = up(max(end - start for start, end in chunks(lons)), LANES)
    row = lax.broadcasted_iota(jnp.int32, (waves, 1), 0)
    m = jnp.zeros((waves, 1), F32)
    for w in range(waves):
        m = jnp.where(row == w, ids_ref[w].astype(F32), m)
    lane = lax.broadcasted_iota(jnp.int32, (1, widest), 1).astype(F32)
    for j in range(rows_here):
        p = pts_ref[j].astype(F32)
        inv_p = 1.0 / jnp.full((1, 1), p, F32)
        weight = jnp.where(2.0 * m < p, jnp.where(m == 0.0, 1.0, 2.0), 0.0)
        cb, sb = turn(m, lane, p, inv_p)
        for start, end in chunks(lons):
            size = end - start
            ca, sa = turn(m, float(start), p, inv_p)
            ca, sa = ca * weight, sa * weight
            inside = lane < p - float(start)
            cos = jnp.where(inside, ca * cb - sa * sb, 0.0)
            sin = jnp.where(inside, -(sa * cb) - ca * sb, 0.0)
            hi, lo = split(jnp.concatenate([cos, sin], 0))
            out_ref[j, 0, :, start:end] = hi[:, :size]
            out_ref[j, 1, :, start:end] = lo[:, :size]


def grid_kernel(table_ref, got_ref, out_hbm, out_ref, sems):
    here, rows_here, lons = out_ref.shape
    parts = 2 * rows_here
    waves = table_ref.shape[2] // 2
    lev_devices = got_ref.shape[0] // (waves * parts)
    here_up = up(here, 8)
    left = []
    for j in range(rows_here):
        halves = []
        for c in range(2):
            total = None
            for d in range(lev_devices):
                x = got_ref[pl.ds(d * waves * parts + c * rows_here + j, waves, stride=parts), :]
                total = x if total is None else total + x
            halves.append(total)
        hi, lo = split(jnp.concatenate(halves, 0)[:, :here_up])
        left.append(jnp.concatenate([hi, hi, lo], 0))
    copies = []
    for i, (start, end) in enumerate(chunks(lons)):
        for j in range(rows_here):
            hi, lo = table_ref[j, 0, :, start:end], table_ref[j, 1, :, start:end]
            x = dot(left[j], jnp.concatenate([hi, lo, hi], 0), ((0,), (0,)))
            out_ref[:, j, start:end] = x[:here]
        copy = pltpu.make_async_copy(
            out_ref.at[:, :, start:end], out_hbm.at[:, :, start:end], sems.at[i]
        )
        copy.start()
        copies.append(copy)
    for copy in copies:
        copy.wait()


def on_device(spectral, to_modes, from_modes, mode_depths, legendre, wave_ids, lat_points):
    lev_devices, waves = lax.axis_size("lev"), lax.axis_size("wave")
    levels, orders = to_modes.shape[0], spectral.shape[3]
    here, rows_here = spectral.shape[1], lat_points.shape[0]
    parts = 2 * rows_here
    vmem = pl.BlockSpec(memory_space=pltpu.VMEM)
    hbm = pl.BlockSpec(memory_space=pltpu.HBM)
    held = (wave_ids, to_modes, mode_depths, legendre, from_modes, spectral)
    blocks = pl.pallas_call(
        functools.partial(send_kernel, lev_devices, waves),
        out_shape=jax.ShapeDtypeStruct((lev_devices * waves * parts, LANES), F32),
        in_specs=[hbm] * 6,
        out_specs=vmem,
        scratch_shapes=[pltpu.SMEM(wave_ids.shape, jnp.int32)]
        + [pltpu.VMEM(x.shape, F32) for x in held[1:]]
        + [
            pltpu.VMEM((up(levels, 16), 3 * up(here, 16)), F32),
            pltpu.VMEM((3, orders // LANES, parts * waves, LANES), F32),
            pltpu.VMEM((up(levels, 16), lev_devices * LANES), F32),
            pltpu.SemaphoreType.DMA((6,)),
        ],
        compiler_params=pltpu.CompilerParams(vmem_limit_bytes=(8 << 20) + 12 * orders * parts * waves * 4),
        name="send",
    )(*(pltpu.with_memory_space_constraint(x, pltpu.HBM) for x in held))
    got = lax.all_to_all(
        blocks.reshape(lev_devices * waves, parts, LANES), ("lev", "wave"), 0, 0, tiled=True
    ).reshape(blocks.shape)
    table_bytes = rows_here * 4 * waves * up(LONS, LANES) * 2
    table = pl.pallas_call(
        table_kernel,
        out_shape=jax.ShapeDtypeStruct((rows_here, 2, 2 * waves, LONS), BF16),
        in_specs=[hbm, hbm],
        out_specs=vmem,
        scratch_shapes=[
            pltpu.SMEM(wave_ids.shape, jnp.int32),
            pltpu.SMEM(lat_points.shape, jnp.int32),
            pltpu.SemaphoreType.DMA((2,)),
        ],
        compiler_params=pltpu.CompilerParams(vmem_limit_bytes=(8 << 20) + 2 * table_bytes),
        name="table",
    )(*(pltpu.with_memory_space_constraint(x, pltpu.HBM) for x in (wave_ids, lat_points)))
    return pl.pallas_call(
        grid_kernel,
        out_shape=jax.ShapeDtypeStruct((here, rows_here, LONS), F32),
        in_specs=[vmem, vmem],
        out_specs=hbm,
        scratch_shapes=[
            pltpu.VMEM((here, rows_here, LONS), F32),
            pltpu.SemaphoreType.DMA((len(chunks(LONS)),)),
        ],
        compiler_params=pltpu.CompilerParams(vmem_limit_bytes=(8 << 20) + 2 * table_bytes),
        name="grid",
    )(table, got)


def solution(mesh):
    return jax.shard_map(
        on_device,
        mesh=mesh,
        in_specs=(
            P("wave", "lev", None, None),
            P(),
            P(),
            P(),
            P("wave", None, None),
            P(),
            P("wave"),
        ),
        out_specs=P("lev", "wave", None),
        check_vma=False,
    )
```

```python
import functools
import math

import jax
import jax.numpy as jnp
from jax import lax
from jax.experimental import pallas as pl
from jax.experimental.pallas import tpu as pltpu
from jax.sharding import PartitionSpec as P

LONS = 5136
LANES = 128
CHUNK = 1280
F32, BF16 = jnp.float32, jnp.bfloat16


def up(size, to):
    return -(-size // to) * to


def split(x):
    hi = x.astype(BF16)
    return hi, (x - hi.astype(F32)).astype(BF16)


def dot(a, b, contract):
    return lax.dot_general(a, b, (contract, ((), ())), preferred_element_type=F32)


def turn(m, i, p, inv_p):
    x = m * i
    r = x - jnp.floor(x * inv_p) * p
    r = jnp.where(r < 0.0, r + p, r)
    r = jnp.where(r >= p, r - p, r)
    quarter = jnp.floor(4.0 * r * inv_p + 0.5)
    v = (4.0 * r - quarter * p) * ((math.pi / 2) * inv_p)
    s = v * v
    sin = v + v * s * (-1.0 / 6 + s * (1.0 / 120 + s * (-1.0 / 5040 + s * (1.0 / 362880))))
    cos = 1.0 + s * (-0.5 + s * (1.0 / 24 + s * (-1.0 / 720 + s * (1.0 / 40320))))
    odd = (quarter == 1.0) | (quarter == 3.0)
    a, b = jnp.where(odd, sin, cos), jnp.where(odd, cos, sin)
    return (
        jnp.where((quarter == 1.0) | (quarter == 2.0), -a, a),
        jnp.where((quarter == 2.0) | (quarter == 3.0), -b, b),
    )


def chunks(lons):
    starts = list(range(0, lons - CHUNK // 2, CHUNK))
    return list(zip(starts, starts[1:] + [lons]))


def builds_early():
    return lax.axis_index("wave") < lax.axis_size("wave") // 2


def fetch(pairs, sems, first):
    copies = [pltpu.make_async_copy(a, b, sems.at[first + i]) for i, (a, b) in enumerate(pairs)]
    for copy in copies:
        copy.start()
    for copy in copies:
        copy.wait()


def build_table(ids_ref, pts_ref, table_ref):
    rows_here, lons = table_ref.shape[0], table_ref.shape[3]
    waves = table_ref.shape[2] // 2
    widest = up(max(end - start for start, end in chunks(lons)), LANES)
    row = lax.broadcasted_iota(jnp.int32, (waves, 1), 0)
    m = jnp.zeros((waves, 1), F32)
    for w in range(waves):
        m = jnp.where(row == w, ids_ref[w].astype(F32), m)
    lane = lax.broadcasted_iota(jnp.int32, (1, widest), 1).astype(F32)
    for j in range(rows_here):
        p = pts_ref[j].astype(F32)
        inv_p = 1.0 / jnp.full((1, 1), p, F32)
        weight = jnp.where(2.0 * m < p, jnp.where(m == 0.0, 1.0, 2.0), 0.0)
        cb, sb = turn(m, lane, p, inv_p)
        for start, end in chunks(lons):
            size = end - start
            ca, sa = turn(m, float(start), p, inv_p)
            ca, sa = ca * weight, sa * weight
            inside = lane < p - float(start)
            cos = jnp.where(inside, ca * cb - sa * sb, 0.0)
            sin = jnp.where(inside, -(sa * cb) - ca * sb, 0.0)
            hi, lo = split(jnp.concatenate([cos, sin], 0))
            table_ref[j, 0, :, start:end] = hi[:, :size]
            table_ref[j, 1, :, start:end] = lo[:, :size]


def send_kernel(
    lev_devices, waves,
    ids_hbm, to_hbm, depth_hbm, leg_hbm, from_hbm, spec_hbm, pts_hbm,
    out_ref, table_ref,
    ids_ref, to_ref, depth_ref, leg_ref, from_ref, spec_ref, cols_ref, tile_ref, back_ref, pts_ref, sems,
):
    copies = [
        pltpu.make_async_copy(source, target, sems.at[i])
        for i, (source, target) in enumerate(
            (
                (depth_hbm, depth_ref),
                (to_hbm, to_ref),
                (leg_hbm, leg_ref),
                (ids_hbm, ids_ref),
                (spec_hbm, spec_ref),
                (from_hbm, from_ref),
            )
        )
    ]
    for copy in copies:
        copy.start()
    levels = to_ref.shape[0]
    here = levels // lev_devices
    orders = leg_ref.shape[2]
    rows_here = leg_ref.shape[1] // waves
    parts = 2 * rows_here
    modes_up, here_up = up(levels, 16), up(here, 16)
    tiles = orders // LANES
    lev, wave = lax.axis_index("lev"), lax.axis_index("wave")
    cols_ref[...] = jnp.zeros_like(cols_ref)
    back_ref[...] = jnp.zeros_like(back_ref)
    tile_ref[...] = jnp.zeros_like(tile_ref)
    copies[0].wait()

    eye = lax.broadcasted_iota(jnp.int32, (levels, levels), 0) == lax.broadcasted_iota(
        jnp.int32, (levels, levels), 1
    )
    depth = jnp.sum(jnp.where(eye, depth_ref[...][None, :], 0.0), axis=1, keepdims=True)
    depth = jnp.concatenate([depth, jnp.zeros((modes_up - levels, 1), F32)], 0)
    n = lax.broadcasted_iota(jnp.int32, (1, orders), 1)
    nf = n.astype(F32)
    inverse = 1.0 / (1.0 + depth * (nf * (nf + 1.0) / float(orders * orders)))
    copies[1].wait()
    for d in range(lev_devices):

        @pl.when(lev == d)
        def _():
            x = to_ref[:, d * here : (d + 1) * here]
            hi = x.astype(BF16).astype(F32)
            cols_ref[:levels, 0:here] = hi
            cols_ref[:levels, here_up : here_up + here] = hi
            cols_ref[:levels, 2 * here_up : 2 * here_up + here] = x - hi

    cols = cols_ref[...].astype(BF16)
    copies[2].wait()
    copies[3].wait()
    for t in range(tiles):
        tile_ref[2, t, : leg_ref.shape[1]] = leg_ref[0, :, t * LANES : (t + 1) * LANES]
        for j in range(rows_here):
            x = tile_ref[2, t, pl.ds(j, waves, stride=rows_here), :]
            for c in range(2):
                tile_ref[c, t, pl.ds(c * rows_here + j, waves, stride=parts), :] = x
    keep = n >= ids_ref[wave]
    leg = [
        split(jnp.where(keep, jnp.concatenate([tile_ref[c, t] for t in range(tiles)], 1), 0.0))
        for c in range(2)
    ]
    leg_hi = jnp.concatenate([leg[0][0], leg[1][0]], 1)
    leg_lo = jnp.concatenate([leg[0][1], leg[1][1]], 1)
    leg_both = jnp.concatenate([leg_hi, leg_lo], 0)

    @pl.when(builds_early())
    def _():
        fetch(((pts_hbm, pts_ref),), sems, 6)
        build_table(ids_ref, pts_ref, table_ref)

    copies[4].wait()
    modes = []
    for c in range(2):
        hi, lo = split(
            jnp.concatenate([spec_ref[0, :, c, :], jnp.zeros((here_up - here, orders), F32)], 0)
        )
        x = dot(cols, jnp.concatenate([hi, lo, hi], 0), ((1,), (0,)))
        modes.append(split(x * inverse))
    copies[5].wait()
    back = from_ref[...].T
    for d in range(lev_devices):
        back_ref[:levels, d * LANES : d * LANES + here] = back[:, d * here : (d + 1) * here]
    back_hi, back_lo = split(back_ref[...])
    back = jnp.concatenate([back_hi, back_lo, back_hi], 0)
    hi = jnp.concatenate([modes[0][0], modes[1][0]], 1)
    lo = jnp.concatenate([modes[0][1], modes[1][1]], 1)
    x = dot(hi, leg_both, ((1,), (1,)))
    y = dot(lo, leg_hi, ((1,), (1,)))
    width = parts * waves
    hi, lo = split(x[:, :width] + (x[:, width:] + y))
    four = dot(jnp.concatenate([hi, hi, lo], 0), back, ((0,), (0,)))
    for d in range(lev_devices):
        out_ref[d * width : (d + 1) * width, :] = four[:, d * LANES : (d + 1) * LANES]


def grid_kernel(first_ref, got_ref, ids_hbm, pts_hbm, out_hbm, out_ref, table_ref, ids_ref, pts_ref, sems):
    early = builds_early()

    @pl.when(early)
    def _():
        table_ref[...] = first_ref[...]

    @pl.when(jnp.logical_not(early))
    def _():
        fetch(((ids_hbm, ids_ref), (pts_hbm, pts_ref)), sems, 0)
        build_table(ids_ref, pts_ref, table_ref)

    here, rows_here, lons = out_ref.shape
    parts = 2 * rows_here
    waves = table_ref.shape[2] // 2
    lev_devices = got_ref.shape[0] // (waves * parts)
    here_up = up(here, 8)
    left = []
    for j in range(rows_here):
        halves = []
        for c in range(2):
            total = None
            for d in range(lev_devices):
                x = got_ref[pl.ds(d * waves * parts + c * rows_here + j, waves, stride=parts), :]
                total = x if total is None else total + x
            halves.append(total)
        hi, lo = split(jnp.concatenate(halves, 0)[:, :here_up])
        left.append(jnp.concatenate([hi, hi, lo], 0))
    copies = []
    for i, (start, end) in enumerate(chunks(lons)):
        for j in range(rows_here):
            hi, lo = table_ref[j, 0, :, start:end], table_ref[j, 1, :, start:end]
            x = dot(left[j], jnp.concatenate([hi, lo, hi], 0), ((0,), (0,)))
            out_ref[:, j, start:end] = x[:here]
        copy = pltpu.make_async_copy(
            out_ref.at[:, :, start:end], out_hbm.at[:, :, start:end], sems.at[i]
        )
        copy.start()
        copies.append(copy)
    for copy in copies:
        copy.wait()


def on_device(spectral, to_modes, from_modes, mode_depths, legendre, wave_ids, lat_points):
    lev_devices, waves = lax.axis_size("lev"), lax.axis_size("wave")
    levels, orders = to_modes.shape[0], spectral.shape[3]
    here, rows_here = spectral.shape[1], lat_points.shape[0]
    parts = 2 * rows_here
    vmem, hbm = pl.BlockSpec(memory_space=pltpu.VMEM), pl.BlockSpec(memory_space=pl.ANY)
    table = jax.ShapeDtypeStruct((rows_here, 2, 2 * waves, LONS), BF16)
    table_bytes = table.size * 2
    spectral, to_modes, from_modes, mode_depths, legendre, wave_ids, lat_points = (
        pltpu.with_memory_space_constraint(x, pltpu.HBM)
        for x in (spectral, to_modes, from_modes, mode_depths, legendre, wave_ids, lat_points)
    )
    ids = [pltpu.SMEM(wave_ids.shape, jnp.int32), pltpu.SMEM(lat_points.shape, jnp.int32)]
    held = (to_modes, mode_depths, legendre, from_modes, spectral)
    blocks, first = pl.pallas_call(
        functools.partial(send_kernel, lev_devices, waves),
        out_shape=(jax.ShapeDtypeStruct((lev_devices * waves * parts, LANES), F32), table),
        in_specs=[hbm] * 7,
        out_specs=(vmem, vmem),
        scratch_shapes=[ids[0]]
        + [pltpu.VMEM(x.shape, F32) for x in held]
        + [
            pltpu.VMEM((up(levels, 16), 3 * up(here, 16)), F32),
            pltpu.VMEM((3, orders // LANES, parts * waves, LANES), F32),
            pltpu.VMEM((up(levels, 16), lev_devices * LANES), F32),
            ids[1],
            pltpu.SemaphoreType.DMA((7,)),
        ],
        compiler_params=pltpu.CompilerParams(
            vmem_limit_bytes=(8 << 20) + 12 * orders * parts * waves * 4 + 2 * table_bytes
        ),
        name="send",
    )(wave_ids, *held, lat_points)
    got = lax.all_to_all(
        blocks.reshape(lev_devices * waves, parts, LANES), ("lev", "wave"), 0, 0, tiled=True
    ).reshape(blocks.shape)
    return pl.pallas_call(
        grid_kernel,
        out_shape=jax.ShapeDtypeStruct((here, rows_here, LONS), F32),
        in_specs=[vmem, vmem, hbm, hbm],
        out_specs=hbm,
        scratch_shapes=[
            pltpu.VMEM((here, rows_here, LONS), F32),
            pltpu.VMEM(table.shape, BF16),
            *ids,
            pltpu.SemaphoreType.DMA((max(2, len(chunks(LONS))),)),
        ],
        compiler_params=pltpu.CompilerParams(vmem_limit_bytes=(8 << 20) + 3 * table_bytes),
        name="grid",
    )(first, got, wave_ids, lat_points)


def solution(mesh):
    return jax.shard_map(
        on_device,
        mesh=mesh,
        in_specs=(
            P("wave", "lev", None, None),
            P(),
            P(),
            P(),
            P("wave", None, None),
            P(),
            P("wave"),
        ),
        out_specs=P("lev", "wave", None),
        check_vma=False,
    )
```

```python
import functools
import math

import jax
import jax.numpy as jnp
from jax import lax
from jax.experimental import pallas as pl
from jax.experimental.pallas import tpu as pltpu
from jax.sharding import PartitionSpec as P

LONS = 5136
LANES = 128
CHUNK = 1280
FIRST = 640
F32, BF16 = jnp.float32, jnp.bfloat16


def up(size, to):
    return -(-size // to) * to


def split(x):
    hi = x.astype(BF16)
    return hi, (x - hi.astype(F32)).astype(BF16)


def dot(a, b, contract):
    return lax.dot_general(a, b, (contract, ((), ())), preferred_element_type=F32)


def turn(m, i, p, inv_p):
    x = m * i
    r = x - jnp.floor(x * inv_p) * p
    r = jnp.where(r < 0.0, r + p, r)
    r = jnp.where(r >= p, r - p, r)
    quarter = jnp.floor(4.0 * r * inv_p + 0.5)
    v = (4.0 * r - quarter * p) * ((math.pi / 2) * inv_p)
    s = v * v
    sin = v + v * s * (-1.0 / 6 + s * (1.0 / 120 + s * (-1.0 / 5040 + s * (1.0 / 362880))))
    cos = 1.0 + s * (-0.5 + s * (1.0 / 24 + s * (-1.0 / 720 + s * (1.0 / 40320))))
    odd = (quarter == 1.0) | (quarter == 3.0)
    a, b = jnp.where(odd, sin, cos), jnp.where(odd, cos, sin)
    return (
        jnp.where((quarter == 1.0) | (quarter == 2.0), -a, a),
        jnp.where((quarter == 2.0) | (quarter == 3.0), -b, b),
    )


def chunks(lons, first=0):
    starts = list(range(0, lons - CHUNK // 2, CHUNK))
    if first:
        starts.insert(1, first)
    return list(zip(starts, starts[1:] + [lons]))


def builds_early():
    return lax.axis_index("wave") < lax.axis_size("wave") // 2


def fetch(pairs, sems, first):
    copies = [pltpu.make_async_copy(a, b, sems.at[first + i]) for i, (a, b) in enumerate(pairs)]
    for copy in copies:
        copy.start()
    for copy in copies:
        copy.wait()


def build_table(ids_ref, pts_ref, table_ref):
    rows_here, lons = table_ref.shape[0], table_ref.shape[3]
    waves = table_ref.shape[2] // 2
    widest = up(max(end - start for start, end in chunks(lons)), LANES)
    row = lax.broadcasted_iota(jnp.int32, (waves, 1), 0)
    m = jnp.zeros((waves, 1), F32)
    for w in range(waves):
        m = jnp.where(row == w, ids_ref[w].astype(F32), m)
    lane = lax.broadcasted_iota(jnp.int32, (1, widest), 1).astype(F32)
    for j in range(rows_here):
        p = pts_ref[j].astype(F32)
        inv_p = 1.0 / jnp.full((1, 1), p, F32)
        weight = jnp.where(2.0 * m < p, jnp.where(m == 0.0, 1.0, 2.0), 0.0)
        cb, sb = turn(m, lane, p, inv_p)
        for start, end in chunks(lons):
            size = end - start
            ca, sa = turn(m, float(start), p, inv_p)
            ca, sa = ca * weight, sa * weight
            inside = lane < p - float(start)
            cos = jnp.where(inside, ca * cb - sa * sb, 0.0)
            sin = jnp.where(inside, -(sa * cb) - ca * sb, 0.0)
            hi, lo = split(jnp.concatenate([cos, sin], 0))
            table_ref[j, 0, :, start:end] = hi[:, :size]
            table_ref[j, 1, :, start:end] = lo[:, :size]


def send_kernel(
    lev_devices, waves,
    ids_hbm, to_hbm, depth_hbm, leg_hbm, from_hbm, spec_hbm, pts_hbm,
    out_ref, table_ref, limit_ref, grid_hbm,
    ids_ref, to_ref, depth_ref, leg_ref, from_ref, spec_ref, cols_ref, tile_ref, back_ref, pts_ref, zero_ref, sems,
):
    copies = [
        pltpu.make_async_copy(source, target, sems.at[i])
        for i, (source, target) in enumerate(
            (
                (depth_hbm, depth_ref),
                (to_hbm, to_ref),
                (leg_hbm, leg_ref),
                (ids_hbm, ids_ref),
                (spec_hbm, spec_ref),
                (from_hbm, from_ref),
            )
        )
    ]
    for copy in copies:
        copy.start()
    levels = to_ref.shape[0]
    here = levels // lev_devices
    orders = leg_ref.shape[2]
    rows_here = leg_ref.shape[1] // waves
    parts = 2 * rows_here
    modes_up, here_up = up(levels, 16), up(here, 16)
    tiles = orders // LANES
    lev, wave = lax.axis_index("lev"), lax.axis_index("wave")
    cols_ref[...] = jnp.zeros_like(cols_ref)
    back_ref[...] = jnp.zeros_like(back_ref)
    tile_ref[...] = jnp.zeros_like(tile_ref)
    copies[0].wait()

    eye = lax.broadcasted_iota(jnp.int32, (levels, levels), 0) == lax.broadcasted_iota(
        jnp.int32, (levels, levels), 1
    )
    depth = jnp.sum(jnp.where(eye, depth_ref[...][None, :], 0.0), axis=1, keepdims=True)
    depth = jnp.concatenate([depth, jnp.zeros((modes_up - levels, 1), F32)], 0)
    n = lax.broadcasted_iota(jnp.int32, (1, orders), 1)
    nf = n.astype(F32)
    inverse = 1.0 / (1.0 + depth * (nf * (nf + 1.0) / float(orders * orders)))
    copies[1].wait()
    for d in range(lev_devices):

        @pl.when(lev == d)
        def _():
            x = to_ref[:, d * here : (d + 1) * here]
            hi = x.astype(BF16).astype(F32)
            cols_ref[:levels, 0:here] = hi
            cols_ref[:levels, here_up : here_up + here] = hi
            cols_ref[:levels, 2 * here_up : 2 * here_up + here] = x - hi

    cols = cols_ref[...].astype(BF16)
    copies[2].wait()
    copies[3].wait()
    for t in range(tiles):
        tile_ref[2, t, : leg_ref.shape[1]] = leg_ref[0, :, t * LANES : (t + 1) * LANES]
        for j in range(rows_here):
            x = tile_ref[2, t, pl.ds(j, waves, stride=rows_here), :]
            for c in range(2):
                tile_ref[c, t, pl.ds(c * rows_here + j, waves, stride=parts), :] = x
    keep = n >= ids_ref[wave]
    leg = [
        split(jnp.where(keep, jnp.concatenate([tile_ref[c, t] for t in range(tiles)], 1), 0.0))
        for c in range(2)
    ]
    leg_hi = jnp.concatenate([leg[0][0], leg[1][0]], 1)
    leg_lo = jnp.concatenate([leg[0][1], leg[1][1]], 1)
    leg_both = jnp.concatenate([leg_hi, leg_lo], 0)

    early = builds_early()
    lons = table_ref.shape[3]
    clears = [
        pltpu.make_async_copy(
            zero_ref.at[:, :, : end - start], grid_hbm.at[:, :, start:end], sems.at[7 + i]
        )
        for i, (start, end) in enumerate(chunks(lons))
    ]

    @pl.when(early)
    def _():
        zero_ref[...] = jnp.zeros_like(zero_ref)
        for clear in clears:
            clear.start()
        fetch(((pts_hbm, pts_ref),), sems, 6)
        longest = pts_ref[0]
        for j in range(1, rows_here):
            longest = jnp.maximum(longest, pts_ref[j])
        limit_ref[...] = jnp.full(limit_ref.shape, longest, jnp.int32).astype(F32)
        build_table(ids_ref, pts_ref, table_ref)

    copies[4].wait()
    modes = []
    for c in range(2):
        hi, lo = split(
            jnp.concatenate([spec_ref[0, :, c, :], jnp.zeros((here_up - here, orders), F32)], 0)
        )
        x = dot(cols, jnp.concatenate([hi, lo, hi], 0), ((1,), (0,)))
        modes.append(split(x * inverse))
    copies[5].wait()
    back = from_ref[...].T
    for d in range(lev_devices):
        back_ref[:levels, d * LANES : d * LANES + here] = back[:, d * here : (d + 1) * here]
    back_hi, back_lo = split(back_ref[...])
    back = jnp.concatenate([back_hi, back_lo, back_hi], 0)
    hi = jnp.concatenate([modes[0][0], modes[1][0]], 1)
    lo = jnp.concatenate([modes[0][1], modes[1][1]], 1)
    x = dot(hi, leg_both, ((1,), (1,)))
    y = dot(lo, leg_hi, ((1,), (1,)))
    width = parts * waves
    hi, lo = split(x[:, :width] + (x[:, width:] + y))
    four = dot(jnp.concatenate([hi, hi, lo], 0), back, ((0,), (0,)))
    for d in range(lev_devices):
        out_ref[d * width : (d + 1) * width, :] = four[:, d * LANES : (d + 1) * LANES]

    @pl.when(early)
    def _():
        for clear in clears:
            clear.wait()


def grid_kernel(
    first_ref, limit_ref, got_ref, ids_hbm, pts_hbm, cleared_hbm,
    out_hbm,
    out_ref, table_ref, ids_ref, pts_ref, sems,
):
    here, rows_here, lons = out_ref.shape
    parts = 2 * rows_here
    waves = table_ref.shape[2] // 2
    lev_devices = got_ref.shape[0] // (waves * parts)
    here_up = up(here, 8)
    early = builds_early()

    def left_sides():
        left = []
        for j in range(rows_here):
            halves = []
            for c in range(2):
                total = None
                for d in range(lev_devices):
                    x = got_ref[pl.ds(d * waves * parts + c * rows_here + j, waves, stride=parts), :]
                    total = x if total is None else total + x
                halves.append(total)
            hi, lo = split(jnp.concatenate(halves, 0)[:, :here_up])
            left.append(jnp.concatenate([hi, hi, lo], 0))
        return left

    def fill(ref, left, start, end):
        for j in range(rows_here):
            hi, lo = ref[j, 0, :, start:end], ref[j, 1, :, start:end]
            x = dot(left[j], jnp.concatenate([hi, lo, hi], 0), ((0,), (0,)))
            out_ref[:, j, start:end] = x[:here]

    def copy(i, start, end):
        return pltpu.make_async_copy(
            out_ref.at[:, :, start:end], out_hbm.at[:, :, start:end], sems.at[i]
        )

    @pl.when(early)
    def _():
        left = left_sides()
        limit = jnp.max(limit_ref[...]).astype(jnp.int32)
        parts_of = chunks(lons, FIRST)
        for i, (start, end) in enumerate(parts_of):

            def one():
                fill(first_ref, left, start, end)
                copy(i, start, end).start()

            one() if i == 0 else pl.when(start < limit)(one)
        for i, (start, end) in enumerate(parts_of):

            def done():
                copy(i, start, end).wait()

            done() if i == 0 else pl.when(start < limit)(done)

    @pl.when(jnp.logical_not(early))
    def _():
        fetch(((ids_hbm, ids_ref), (pts_hbm, pts_ref)), sems, 0)
        build_table(ids_ref, pts_ref, table_ref)
        left = left_sides()
        for i, (start, end) in enumerate(chunks(lons)):
            fill(table_ref, left, start, end)
            copy(i, start, end).start()
        for i, (start, end) in enumerate(chunks(lons)):
            copy(i, start, end).wait()


def on_device(spectral, to_modes, from_modes, mode_depths, legendre, wave_ids, lat_points):
    lev_devices, waves = lax.axis_size("lev"), lax.axis_size("wave")
    levels, orders = to_modes.shape[0], spectral.shape[3]
    here, rows_here = spectral.shape[1], lat_points.shape[0]
    parts = 2 * rows_here
    vmem, hbm = pl.BlockSpec(memory_space=pltpu.VMEM), pl.BlockSpec(memory_space=pl.ANY)
    table = jax.ShapeDtypeStruct((rows_here, 2, 2 * waves, LONS), BF16)
    table_bytes = table.size * 2
    spectral, to_modes, from_modes, mode_depths, legendre, wave_ids, lat_points = (
        pltpu.with_memory_space_constraint(x, pltpu.HBM)
        for x in (spectral, to_modes, from_modes, mode_depths, legendre, wave_ids, lat_points)
    )
    widest = max(end - start for start, end in chunks(LONS))
    ids = [pltpu.SMEM(wave_ids.shape, jnp.int32), pltpu.SMEM(lat_points.shape, jnp.int32)]
    held = (to_modes, mode_depths, legendre, from_modes, spectral)
    grid = jax.ShapeDtypeStruct((here, rows_here, LONS), F32)
    blocks, first, limit, cleared = pl.pallas_call(
        functools.partial(send_kernel, lev_devices, waves),
        out_shape=(
            jax.ShapeDtypeStruct((lev_devices * waves * parts, LANES), F32),
            table,
            jax.ShapeDtypeStruct((8, LANES), F32),
            grid,
        ),
        in_specs=[hbm] * 7,
        out_specs=(vmem, vmem, vmem, hbm),
        scratch_shapes=[ids[0]]
        + [pltpu.VMEM(x.shape, F32) for x in held]
        + [
            pltpu.VMEM((up(levels, 16), 3 * up(here, 16)), F32),
            pltpu.VMEM((3, orders // LANES, parts * waves, LANES), F32),
            pltpu.VMEM((up(levels, 16), lev_devices * LANES), F32),
            ids[1],
            pltpu.VMEM((here, rows_here, widest), F32),
            pltpu.SemaphoreType.DMA((7 + len(chunks(LONS)),)),
        ],
        compiler_params=pltpu.CompilerParams(
            vmem_limit_bytes=(8 << 20) + 12 * orders * parts * waves * 4 + 2 * table_bytes
        ),
        name="send",
    )(wave_ids, *held, lat_points)
    got = lax.all_to_all(
        blocks.reshape(lev_devices * waves, parts, LANES), ("lev", "wave"), 0, 0, tiled=True
    ).reshape(blocks.shape)
    return pl.pallas_call(
        grid_kernel,
        out_shape=grid,
        in_specs=[vmem, vmem, vmem, hbm, hbm, hbm],
        input_output_aliases={5: 0},
        out_specs=hbm,
        scratch_shapes=[
            pltpu.VMEM((here, rows_here, LONS), F32),
            pltpu.VMEM(table.shape, BF16),
            *ids,
            pltpu.SemaphoreType.DMA((len(chunks(LONS, FIRST)),)),
        ],
        compiler_params=pltpu.CompilerParams(vmem_limit_bytes=(8 << 20) + 3 * table_bytes),
        name="grid",
    )(first, limit, got, wave_ids, lat_points, cleared)


def solution(mesh):
    return jax.shard_map(
        on_device,
        mesh=mesh,
        in_specs=(
            P("wave", "lev", None, None),
            P(),
            P(),
            P(),
            P("wave", None, None),
            P(),
            P("wave"),
        ),
        out_specs=P("lev", "wave", None),
        check_vma=False,
    )
```

```python
import functools
import math

import jax
import jax.numpy as jnp
from jax import lax
from jax.experimental import pallas as pl
from jax.experimental.pallas import tpu as pltpu
from jax.sharding import PartitionSpec as P

LONS = 5136
LANES = 128
CHUNK = 1280
FIRST = 640
TAILS = (2, 5)
F32, BF16 = jnp.float32, jnp.bfloat16


def up(size, to):
    return -(-size // to) * to


def split(x):
    hi = x.astype(BF16)
    return hi, (x - hi.astype(F32)).astype(BF16)


def dot(a, b, contract):
    return lax.dot_general(a, b, (contract, ((), ())), preferred_element_type=F32)


def turn(m, i, p, inv_p):
    x = m * i
    r = x - jnp.floor(x * inv_p) * p
    r = jnp.where(r < 0.0, r + p, r)
    r = jnp.where(r >= p, r - p, r)
    quarter = jnp.floor(4.0 * r * inv_p + 0.5)
    v = (4.0 * r - quarter * p) * ((math.pi / 2) * inv_p)
    s = v * v
    sin = v + v * s * (-1.0 / 6 + s * (1.0 / 120 + s * (-1.0 / 5040 + s * (1.0 / 362880))))
    cos = 1.0 + s * (-0.5 + s * (1.0 / 24 + s * (-1.0 / 720 + s * (1.0 / 40320))))
    odd = (quarter == 1.0) | (quarter == 3.0)
    a, b = jnp.where(odd, sin, cos), jnp.where(odd, cos, sin)
    return (
        jnp.where((quarter == 1.0) | (quarter == 2.0), -a, a),
        jnp.where((quarter == 2.0) | (quarter == 3.0), -b, b),
    )


def chunks(lons, first=0):
    starts = list(range(0, lons - CHUNK // 2, CHUNK))
    if first:
        starts.insert(1, first)
    return list(zip(starts, starts[1:] + [lons]))


def builds_early():
    return lax.axis_index("wave") < lax.axis_size("wave") // 4


def fetch(pairs, sems, first):
    copies = [pltpu.make_async_copy(a, b, sems.at[first + i]) for i, (a, b) in enumerate(pairs)]
    for copy in copies:
        copy.start()
    for copy in copies:
        copy.wait()


def build_table(ids_ref, pts_ref, table_ref):
    rows_here, lons = table_ref.shape[0], table_ref.shape[3]
    waves = table_ref.shape[2] // 2
    widest = up(max(end - start for start, end in chunks(lons)), LANES)
    row = lax.broadcasted_iota(jnp.int32, (waves, 1), 0)
    m = jnp.zeros((waves, 1), F32)
    for w in range(waves):
        m = jnp.where(row == w, ids_ref[w].astype(F32), m)
    lane = lax.broadcasted_iota(jnp.int32, (1, widest), 1).astype(F32)
    for j in range(rows_here):
        p = pts_ref[j].astype(F32)
        inv_p = 1.0 / jnp.full((1, 1), p, F32)
        weight = jnp.where(2.0 * m < p, jnp.where(m == 0.0, 1.0, 2.0), 0.0)
        cb, sb = turn(m, lane, p, inv_p)
        for start, end in chunks(lons):
            size = end - start
            ca, sa = turn(m, float(start), p, inv_p)
            ca, sa = ca * weight, sa * weight
            inside = lane < p - float(start)
            cos = jnp.where(inside, ca * cb - sa * sb, 0.0)
            sin = jnp.where(inside, -(sa * cb) - ca * sb, 0.0)
            hi, lo = split(jnp.concatenate([cos, sin], 0))
            table_ref[j, 0, :, start:end] = hi[:, :size]
            table_ref[j, 1, :, start:end] = lo[:, :size]


def send_kernel(
    lev_devices, waves,
    ids_hbm, to_hbm, depth_hbm, leg_hbm, from_hbm, spec_hbm, pts_hbm,
    out_ref, table_ref, limit_ref, grid_hbm,
    ids_ref, to_ref, depth_ref, leg_ref, from_ref, spec_ref, cols_ref, tile_ref, back_ref, pts_ref, zero_ref, sems,
):
    copies = [
        pltpu.make_async_copy(source, target, sems.at[i])
        for i, (source, target) in enumerate(
            (
                (depth_hbm, depth_ref),
                (to_hbm, to_ref),
                (leg_hbm, leg_ref),
                (ids_hbm, ids_ref),
                (spec_hbm, spec_ref),
                (from_hbm, from_ref),
            )
        )
    ]
    for copy in copies:
        copy.start()
    levels = to_ref.shape[0]
    here = levels // lev_devices
    orders = leg_ref.shape[2]
    rows_here = leg_ref.shape[1] // waves
    parts = 2 * rows_here
    modes_up, here_up = up(levels, 16), up(here, 16)
    lev, wave = lax.axis_index("lev"), lax.axis_index("wave")
    cols_ref[...] = jnp.zeros_like(cols_ref)
    back_ref[...] = jnp.zeros_like(back_ref)
    tile_ref[...] = jnp.zeros_like(tile_ref)
    copies[0].wait()

    eye = lax.broadcasted_iota(jnp.int32, (levels, levels), 0) == lax.broadcasted_iota(
        jnp.int32, (levels, levels), 1
    )
    depth = jnp.sum(jnp.where(eye, depth_ref[...][None, :], 0.0), axis=1, keepdims=True)
    depth = jnp.concatenate([depth, jnp.zeros((modes_up - levels, 1), F32)], 0)
    copies[1].wait()
    for d in range(lev_devices):

        @pl.when(lev == d)
        def _():
            x = to_ref[:, d * here : (d + 1) * here]
            hi = x.astype(BF16).astype(F32)
            cols_ref[:levels, 0:here] = hi
            cols_ref[:levels, here_up : here_up + here] = hi
            cols_ref[:levels, 2 * here_up : 2 * here_up + here] = x - hi

    copies[2].wait()
    copies[3].wait()
    own = ids_ref[wave]

    early = builds_early()
    lons = table_ref.shape[3]
    clears = [
        pltpu.make_async_copy(
            zero_ref.at[:, :, : end - start], grid_hbm.at[:, :, start:end], sems.at[7 + i]
        )
        for i, (start, end) in enumerate(chunks(lons))
    ]

    @pl.when(early)
    def _():
        zero_ref[...] = jnp.zeros_like(zero_ref)
        for clear in clears:
            clear.start()
        fetch(((pts_hbm, pts_ref),), sems, 6)
        longest = pts_ref[0]
        for j in range(1, rows_here):
            longest = jnp.maximum(longest, pts_ref[j])
        limit_ref[...] = jnp.full(limit_ref.shape, longest, jnp.int32).astype(F32)
        build_table(ids_ref, pts_ref, table_ref)

    def solve(low):
        tiles = range(low // LANES, orders // LANES)
        n = low + lax.broadcasted_iota(jnp.int32, (1, orders - low), 1)
        nf = n.astype(F32)
        inverse = 1.0 / (1.0 + depth * (nf * (nf + 1.0) / float(orders * orders)))
        cols = cols_ref[...].astype(BF16)
        for t in tiles:
            tile_ref[2, t, : leg_ref.shape[1]] = leg_ref[0, :, t * LANES : (t + 1) * LANES]
            for j in range(rows_here):
                x = tile_ref[2, t, pl.ds(j, waves, stride=rows_here), :]
                for c in range(2):
                    tile_ref[c, t, pl.ds(c * rows_here + j, waves, stride=parts), :] = x
        keep = n >= own
        leg = [
            split(jnp.where(keep, jnp.concatenate([tile_ref[c, t] for t in tiles], 1), 0.0))
            for c in range(2)
        ]
        leg_hi = jnp.concatenate([leg[0][0], leg[1][0]], 1)
        leg_lo = jnp.concatenate([leg[0][1], leg[1][1]], 1)
        leg_both = jnp.concatenate([leg_hi, leg_lo], 0)
        copies[4].wait()
        modes = []
        for c in range(2):
            zero = jnp.zeros((here_up - here, orders - low), F32)
            hi, lo = split(jnp.concatenate([spec_ref[0, :, c, low:], zero], 0))
            x = dot(cols, jnp.concatenate([hi, lo, hi], 0), ((1,), (0,)))
            modes.append(split(x * inverse))
        copies[5].wait()
        back = from_ref[...].T
        for d in range(lev_devices):
            back_ref[:levels, d * LANES : d * LANES + here] = back[:, d * here : (d + 1) * here]
        back_hi, back_lo = split(back_ref[...])
        back = jnp.concatenate([back_hi, back_lo, back_hi], 0)
        hi = jnp.concatenate([modes[0][0], modes[1][0]], 1)
        lo = jnp.concatenate([modes[0][1], modes[1][1]], 1)
        x = dot(hi, leg_both, ((1,), (1,)))
        y = dot(lo, leg_hi, ((1,), (1,)))
        width = parts * waves
        hi, lo = split(x[:, :width] + (x[:, width:] + y))
        four = dot(jnp.concatenate([hi, hi, lo], 0), back, ((0,), (0,)))
        for d in range(lev_devices):
            out_ref[d * width : (d + 1) * width, :] = four[:, d * LANES : (d + 1) * LANES]

    lows = [0] + [orders - up(orders // share, LANES) for share in TAILS]
    for low, above in zip(lows, lows[1:] + [orders]):
        pl.when((own >= low) & (own < above))(functools.partial(solve, low))

    @pl.when(early)
    def _():
        for clear in clears:
            clear.wait()


def grid_kernel(
    first_ref, limit_ref, got_ref, ids_hbm, pts_hbm, cleared_hbm,
    out_hbm,
    out_ref, table_ref, ids_ref, pts_ref, sems,
):
    here, rows_here, lons = out_ref.shape
    parts = 2 * rows_here
    waves = table_ref.shape[2] // 2
    lev_devices = got_ref.shape[0] // (waves * parts)
    here_up = up(here, 8)
    early = builds_early()

    def left_sides():
        left = []
        for j in range(rows_here):
            halves = []
            for c in range(2):
                total = None
                for d in range(lev_devices):
                    x = got_ref[pl.ds(d * waves * parts + c * rows_here + j, waves, stride=parts), :]
                    total = x if total is None else total + x
                halves.append(total)
            hi, lo = split(jnp.concatenate(halves, 0)[:, :here_up])
            left.append(jnp.concatenate([hi, hi, lo], 0))
        return left

    def fill(ref, left, start, end):
        for j in range(rows_here):
            hi, lo = ref[j, 0, :, start:end], ref[j, 1, :, start:end]
            x = dot(left[j], jnp.concatenate([hi, lo, hi], 0), ((0,), (0,)))
            out_ref[:, j, start:end] = x[:here]

    def copy(i, start, end):
        return pltpu.make_async_copy(
            out_ref.at[:, :, start:end], out_hbm.at[:, :, start:end], sems.at[i]
        )

    @pl.when(early)
    def _():
        left = left_sides()
        limit = jnp.max(limit_ref[...]).astype(jnp.int32)
        parts_of = chunks(lons, FIRST)
        for i, (start, end) in enumerate(parts_of):

            def one():
                fill(first_ref, left, start, end)
                copy(i, start, end).start()

            one() if i == 0 else pl.when(start < limit)(one)
        for i, (start, end) in enumerate(parts_of):

            def done():
                copy(i, start, end).wait()

            done() if i == 0 else pl.when(start < limit)(done)

    @pl.when(jnp.logical_not(early))
    def _():
        fetch(((ids_hbm, ids_ref), (pts_hbm, pts_ref)), sems, 0)
        build_table(ids_ref, pts_ref, table_ref)
        left = left_sides()
        for i, (start, end) in enumerate(chunks(lons)):
            fill(table_ref, left, start, end)
            copy(i, start, end).start()
        for i, (start, end) in enumerate(chunks(lons)):
            copy(i, start, end).wait()


def on_device(spectral, to_modes, from_modes, mode_depths, legendre, wave_ids, lat_points):
    lev_devices, waves = lax.axis_size("lev"), lax.axis_size("wave")
    levels, orders = to_modes.shape[0], spectral.shape[3]
    here, rows_here = spectral.shape[1], lat_points.shape[0]
    parts = 2 * rows_here
    vmem, hbm = pl.BlockSpec(memory_space=pltpu.VMEM), pl.BlockSpec(memory_space=pl.ANY)
    table = jax.ShapeDtypeStruct((rows_here, 2, 2 * waves, LONS), BF16)
    table_bytes = table.size * 2
    spectral, to_modes, from_modes, mode_depths, legendre, wave_ids, lat_points = (
        pltpu.with_memory_space_constraint(x, pltpu.HBM)
        for x in (spectral, to_modes, from_modes, mode_depths, legendre, wave_ids, lat_points)
    )
    widest = max(end - start for start, end in chunks(LONS))
    ids = [pltpu.SMEM(wave_ids.shape, jnp.int32), pltpu.SMEM(lat_points.shape, jnp.int32)]
    held = (to_modes, mode_depths, legendre, from_modes, spectral)
    grid = jax.ShapeDtypeStruct((here, rows_here, LONS), F32)
    blocks, first, limit, cleared = pl.pallas_call(
        functools.partial(send_kernel, lev_devices, waves),
        out_shape=(
            jax.ShapeDtypeStruct((lev_devices * waves * parts, LANES), F32),
            table,
            jax.ShapeDtypeStruct((8, LANES), F32),
            grid,
        ),
        in_specs=[hbm] * 7,
        out_specs=(vmem, vmem, vmem, hbm),
        scratch_shapes=[ids[0]]
        + [pltpu.VMEM(x.shape, F32) for x in held]
        + [
            pltpu.VMEM((up(levels, 16), 3 * up(here, 16)), F32),
            pltpu.VMEM((3, orders // LANES, parts * waves, LANES), F32),
            pltpu.VMEM((up(levels, 16), lev_devices * LANES), F32),
            ids[1],
            pltpu.VMEM((here, rows_here, widest), F32),
            pltpu.SemaphoreType.DMA((7 + len(chunks(LONS)),)),
        ],
        compiler_params=pltpu.CompilerParams(
            vmem_limit_bytes=(8 << 20) + 12 * orders * parts * waves * 4 + 2 * table_bytes
        ),
        name="send",
    )(wave_ids, *held, lat_points)
    got = lax.all_to_all(
        blocks.reshape(lev_devices * waves, parts, LANES), ("lev", "wave"), 0, 0, tiled=True
    ).reshape(blocks.shape)
    return pl.pallas_call(
        grid_kernel,
        out_shape=grid,
        in_specs=[vmem, vmem, vmem, hbm, hbm, hbm],
        input_output_aliases={5: 0},
        out_specs=hbm,
        scratch_shapes=[
            pltpu.VMEM((here, rows_here, LONS), F32),
            pltpu.VMEM(table.shape, BF16),
            *ids,
            pltpu.SemaphoreType.DMA((len(chunks(LONS, FIRST)),)),
        ],
        compiler_params=pltpu.CompilerParams(vmem_limit_bytes=(8 << 20) + 3 * table_bytes),
        name="grid",
    )(first, limit, got, wave_ids, lat_points, cleared)


def solution(mesh):
    return jax.shard_map(
        on_device,
        mesh=mesh,
        in_specs=(
            P("wave", "lev", None, None),
            P(),
            P(),
            P(),
            P("wave", None, None),
            P(),
            P("wave"),
        ),
        out_specs=P("lev", "wave", None),
        check_vma=False,
    )
```

```python
import functools
import math

import jax
import jax.numpy as jnp
from jax import lax
from jax.experimental import pallas as pl
from jax.experimental.pallas import tpu as pltpu
from jax.sharding import PartitionSpec as P

LONS = 5136
LANES = 128
CHUNK = 1280
FIRST = 1024
TAILS = (5, 4, 3, 2, 1)
SHORT = 512
F32, BF16 = jnp.float32, jnp.bfloat16


def up(size, to):
    return -(-size // to) * to


def split(x):
    hi = x.astype(BF16)
    return hi, (x - hi.astype(F32)).astype(BF16)


def dot(a, b, contract):
    return lax.dot_general(a, b, (contract, ((), ())), preferred_element_type=F32)


def turn(m, i, p, inv_p):
    x = m * i
    r = x - jnp.floor(x * inv_p) * p
    r = jnp.where(r < 0.0, r + p, r)
    r = jnp.where(r >= p, r - p, r)
    quarter = jnp.floor(4.0 * r * inv_p + 0.5)
    v = (4.0 * r - quarter * p) * ((math.pi / 2) * inv_p)
    s = v * v
    sin = v + v * s * (-1.0 / 6 + s * (1.0 / 120 + s * (-1.0 / 5040 + s * (1.0 / 362880))))
    cos = 1.0 + s * (-0.5 + s * (1.0 / 24 + s * (-1.0 / 720 + s * (1.0 / 40320))))
    odd = (quarter == 1.0) | (quarter == 3.0)
    a, b = jnp.where(odd, sin, cos), jnp.where(odd, cos, sin)
    return (
        jnp.where((quarter == 1.0) | (quarter == 2.0), -a, a),
        jnp.where((quarter == 2.0) | (quarter == 3.0), -b, b),
    )


def chunks(lons, first=0):
    starts = list(range(0, lons - CHUNK // 2, CHUNK))
    if first:
        starts.insert(1, first)
    return list(zip(starts, starts[1:] + [lons]))


def builds_early():
    return lax.axis_index("wave") < lax.axis_size("wave") // 4


def fetch(pairs, sems, first):
    copies = [pltpu.make_async_copy(a, b, sems.at[first + i]) for i, (a, b) in enumerate(pairs)]
    for copy in copies:
        copy.start()
    for copy in copies:
        copy.wait()


def build_table(ids_ref, pts_ref, table_ref):
    rows_here, lons = table_ref.shape[0], table_ref.shape[3]
    waves = table_ref.shape[2] // 2
    widest = up(max(end - start for start, end in chunks(lons)), LANES)
    row = lax.broadcasted_iota(jnp.int32, (waves, 1), 0)
    m = jnp.zeros((waves, 1), F32)
    for w in range(waves):
        m = jnp.where(row == w, ids_ref[w].astype(F32), m)
    lane = lax.broadcasted_iota(jnp.int32, (1, widest), 1).astype(F32)
    for j in range(rows_here):
        p = pts_ref[j].astype(F32)
        inv_p = 1.0 / jnp.full((1, 1), p, F32)
        weight = jnp.where(2.0 * m < p, jnp.where(m == 0.0, 1.0, 2.0), 0.0)
        cb, sb = turn(m, lane, p, inv_p)
        for start, end in chunks(lons):
            size = end - start
            ca, sa = turn(m, float(start), p, inv_p)
            ca, sa = ca * weight, sa * weight
            inside = lane < p - float(start)
            cos = jnp.where(inside, ca * cb - sa * sb, 0.0)
            sin = jnp.where(inside, -(sa * cb) - ca * sb, 0.0)
            hi, lo = split(jnp.concatenate([cos, sin], 0))
            table_ref[j, 0, :, start:end] = hi[:, :size]
            table_ref[j, 1, :, start:end] = lo[:, :size]


def send_kernel(
    lev_devices, waves,
    ids_hbm, to_hbm, depth_hbm, leg_hbm, from_hbm, spec_hbm, pts_hbm,
    out_ref, table_ref, limit_ref, grid_hbm,
    ids_ref, to_ref, depth_ref, leg_ref, from_ref, spec_ref, cols_ref, tile_ref, back_ref, pts_ref, zero_ref, sems,
):
    copies = [
        pltpu.make_async_copy(source, target, sems.at[i])
        for i, (source, target) in enumerate(
            (
                (depth_hbm, depth_ref),
                (to_hbm, to_ref),
                (leg_hbm, leg_ref),
                (ids_hbm, ids_ref),
                (spec_hbm, spec_ref),
                (from_hbm, from_ref),
            )
        )
    ]
    for copy in copies:
        copy.start()
    levels = to_ref.shape[0]
    here = levels // lev_devices
    orders = leg_ref.shape[2]
    rows_here = leg_ref.shape[1] // waves
    parts = 2 * rows_here
    modes_up, here_up = up(levels, 16), up(here, 16)
    lev, wave = lax.axis_index("lev"), lax.axis_index("wave")
    cols_ref[...] = jnp.zeros_like(cols_ref)
    back_ref[...] = jnp.zeros_like(back_ref)
    tile_ref[...] = jnp.zeros_like(tile_ref)
    copies[0].wait()

    eye = lax.broadcasted_iota(jnp.int32, (levels, levels), 0) == lax.broadcasted_iota(
        jnp.int32, (levels, levels), 1
    )
    depth = jnp.sum(jnp.where(eye, depth_ref[...][None, :], 0.0), axis=1, keepdims=True)
    depth = jnp.concatenate([depth, jnp.zeros((modes_up - levels, 1), F32)], 0)
    copies[1].wait()
    for d in range(lev_devices):

        @pl.when(lev == d)
        def _():
            x = to_ref[:, d * here : (d + 1) * here]
            hi = x.astype(BF16).astype(F32)
            cols_ref[:levels, 0:here] = hi
            cols_ref[:levels, here_up : here_up + here] = hi
            cols_ref[:levels, 2 * here_up : 2 * here_up + here] = x - hi

    copies[2].wait()
    copies[3].wait()
    own = ids_ref[wave]

    early = builds_early()
    lons = table_ref.shape[3]
    clears = [
        pltpu.make_async_copy(
            zero_ref.at[:, :, : end - start], grid_hbm.at[:, :, start:end], sems.at[7 + i]
        )
        for i, (start, end) in enumerate(chunks(lons))
    ]

    @pl.when(early)
    def _():
        zero_ref[...] = jnp.zeros_like(zero_ref)
        for clear in clears:
            clear.start()
        fetch(((pts_hbm, pts_ref),), sems, 6)
        longest = pts_ref[0]
        for j in range(1, rows_here):
            longest = jnp.maximum(longest, pts_ref[j])
        limit_ref[...] = jnp.full(limit_ref.shape, longest, jnp.int32).astype(F32)
        build_table(ids_ref, pts_ref, table_ref)

    def solve(low):
        tiles = range(low // LANES, orders // LANES)
        n = low + lax.broadcasted_iota(jnp.int32, (1, orders - low), 1)
        nf = n.astype(F32)
        inverse = 1.0 / (1.0 + depth * (nf * (nf + 1.0) / float(orders * orders)))
        cols = cols_ref[...].astype(BF16)
        for t in tiles:
            tile_ref[2, t, : leg_ref.shape[1]] = leg_ref[0, :, t * LANES : (t + 1) * LANES]
            for j in range(rows_here):
                x = tile_ref[2, t, pl.ds(j, waves, stride=rows_here), :]
                for c in range(2):
                    tile_ref[c, t, pl.ds(c * rows_here + j, waves, stride=parts), :] = x
        keep = n >= own
        leg = [
            split(jnp.where(keep, jnp.concatenate([tile_ref[c, t] for t in tiles], 1), 0.0))
            for c in range(2)
        ]
        leg_hi = jnp.concatenate([leg[0][0], leg[1][0]], 1)
        leg_lo = jnp.concatenate([leg[0][1], leg[1][1]], 1)
        copies[4].wait()
        modes = []
        for c in range(2):
            zero = jnp.zeros((here_up - here, orders - low), F32)
            hi, lo = split(jnp.concatenate([spec_ref[0, :, c, low:], zero], 0))
            x = dot(cols, jnp.concatenate([hi, lo, hi], 0), ((1,), (0,)))
            modes.append(split(x * inverse))
        copies[5].wait()
        back = from_ref[...].T
        for d in range(lev_devices):
            back_ref[:levels, d * LANES : d * LANES + here] = back[:, d * here : (d + 1) * here]
        back_hi, back_lo = split(back_ref[...])
        hi = jnp.concatenate([modes[0][0], modes[1][0]], 1)
        lo = jnp.concatenate([modes[0][1], modes[1][1]], 1)
        width = parts * waves
        if orders - low <= SHORT:
            x = dot(
                jnp.concatenate([leg_hi, leg_lo, leg_hi], 1),
                jnp.concatenate([hi, hi, lo], 1),
                ((1,), (1,)),
            )
            hi, lo = split(x)
            x = dot(jnp.concatenate([hi, lo], 0), back_hi, ((1,), (0,)))
            four = x[:width] + (x[width:] + dot(hi, back_lo, ((1,), (0,))))
        else:
            x = dot(hi, jnp.concatenate([leg_hi, leg_lo], 0), ((1,), (1,)))
            y = dot(lo, leg_hi, ((1,), (1,)))
            hi, lo = split(x[:, :width] + (x[:, width:] + y))
            back = jnp.concatenate([back_hi, back_lo, back_hi], 0)
            four = dot(jnp.concatenate([hi, hi, lo], 0), back, ((0,), (0,)))
        for d in range(lev_devices):
            out_ref[d * width : (d + 1) * width, :] = four[:, d * LANES : (d + 1) * LANES]

    lows = [0] + [orders - up(orders * tenths // 10, LANES) for tenths in TAILS]
    for low, above in zip(lows, lows[1:] + [orders]):
        pl.when((own >= low) & (own < above))(functools.partial(solve, low))

    @pl.when(early)
    def _():
        for clear in clears:
            clear.wait()


def grid_kernel(
    first_ref, limit_ref, got_ref, ids_hbm, pts_hbm, cleared_hbm,
    out_hbm,
    out_ref, table_ref, ids_ref, pts_ref, sems,
):
    here, rows_here, lons = out_ref.shape
    parts = 2 * rows_here
    waves = table_ref.shape[2] // 2
    lev_devices = got_ref.shape[0] // (waves * parts)
    here_up = up(here, 8)
    early = builds_early()

    def left_sides():
        left = []
        for j in range(rows_here):
            halves = []
            for c in range(2):
                total = None
                for d in range(lev_devices):
                    x = got_ref[pl.ds(d * waves * parts + c * rows_here + j, waves, stride=parts), :]
                    total = x if total is None else total + x
                halves.append(total)
            hi, lo = split(jnp.concatenate(halves, 0)[:, :here_up])
            left.append(jnp.concatenate([hi, hi, lo], 0))
        return left

    def fill(ref, left, start, end):
        for j in range(rows_here):
            hi, lo = ref[j, 0, :, start:end], ref[j, 1, :, start:end]
            x = dot(left[j], jnp.concatenate([hi, lo, hi], 0), ((0,), (0,)))
            out_ref[:, j, start:end] = x[:here]

    def copy(i, start, end):
        return pltpu.make_async_copy(
            out_ref.at[:, :, start:end], out_hbm.at[:, :, start:end], sems.at[i]
        )

    @pl.when(early)
    def _():
        left = left_sides()
        limit = jnp.max(limit_ref[...]).astype(jnp.int32)
        parts_of = chunks(lons, FIRST)
        for i, (start, end) in enumerate(parts_of):

            def one():
                fill(first_ref, left, start, end)
                copy(i, start, end).start()

            one() if i == 0 else pl.when(start < limit)(one)
        for i, (start, end) in enumerate(parts_of):

            def done():
                copy(i, start, end).wait()

            done() if i == 0 else pl.when(start < limit)(done)

    @pl.when(jnp.logical_not(early))
    def _():
        fetch(((ids_hbm, ids_ref), (pts_hbm, pts_ref)), sems, 0)
        build_table(ids_ref, pts_ref, table_ref)
        left = left_sides()
        for i, (start, end) in enumerate(chunks(lons)):
            fill(table_ref, left, start, end)
            copy(i, start, end).start()
        for i, (start, end) in enumerate(chunks(lons)):
            copy(i, start, end).wait()


def on_device(spectral, to_modes, from_modes, mode_depths, legendre, wave_ids, lat_points):
    lev_devices, waves = lax.axis_size("lev"), lax.axis_size("wave")
    levels, orders = to_modes.shape[0], spectral.shape[3]
    here, rows_here = spectral.shape[1], lat_points.shape[0]
    parts = 2 * rows_here
    vmem, hbm = pl.BlockSpec(memory_space=pltpu.VMEM), pl.BlockSpec(memory_space=pl.ANY)
    table = jax.ShapeDtypeStruct((rows_here, 2, 2 * waves, LONS), BF16)
    table_bytes = table.size * 2
    spectral, to_modes, from_modes, mode_depths, legendre, wave_ids, lat_points = (
        pltpu.with_memory_space_constraint(x, pltpu.HBM)
        for x in (spectral, to_modes, from_modes, mode_depths, legendre, wave_ids, lat_points)
    )
    widest = max(end - start for start, end in chunks(LONS))
    ids = [pltpu.SMEM(wave_ids.shape, jnp.int32), pltpu.SMEM(lat_points.shape, jnp.int32)]
    held = (to_modes, mode_depths, legendre, from_modes, spectral)
    grid = jax.ShapeDtypeStruct((here, rows_here, LONS), F32)
    blocks, first, limit, cleared = pl.pallas_call(
        functools.partial(send_kernel, lev_devices, waves),
        out_shape=(
            jax.ShapeDtypeStruct((lev_devices * waves * parts, LANES), F32),
            table,
            jax.ShapeDtypeStruct((8, LANES), F32),
            grid,
        ),
        in_specs=[hbm] * 7,
        out_specs=(vmem, vmem, vmem, hbm),
        scratch_shapes=[ids[0]]
        + [pltpu.VMEM(x.shape, F32) for x in held]
        + [
            pltpu.VMEM((up(levels, 16), 3 * up(here, 16)), F32),
            pltpu.VMEM((3, orders // LANES, parts * waves, LANES), F32),
            pltpu.VMEM((up(levels, 16), lev_devices * LANES), F32),
            ids[1],
            pltpu.VMEM((here, rows_here, widest), F32),
            pltpu.SemaphoreType.DMA((7 + len(chunks(LONS)),)),
        ],
        compiler_params=pltpu.CompilerParams(
            vmem_limit_bytes=(8 << 20) + 12 * orders * parts * waves * 4 + 2 * table_bytes
        ),
        name="send",
    )(wave_ids, *held, lat_points)
    got = lax.all_to_all(
        blocks.reshape(lev_devices * waves, parts, LANES), ("lev", "wave"), 0, 0, tiled=True
    ).reshape(blocks.shape)
    return pl.pallas_call(
        grid_kernel,
        out_shape=grid,
        in_specs=[vmem, vmem, vmem, hbm, hbm, hbm],
        input_output_aliases={5: 0},
        out_specs=hbm,
        scratch_shapes=[
            pltpu.VMEM((here, rows_here, LONS), F32),
            pltpu.VMEM(table.shape, BF16),
            *ids,
            pltpu.SemaphoreType.DMA((len(chunks(LONS, FIRST)),)),
        ],
        compiler_params=pltpu.CompilerParams(vmem_limit_bytes=(8 << 20) + 3 * table_bytes),
        name="grid",
    )(first, limit, got, wave_ids, lat_points, cleared)


def solution(mesh):
    return jax.shard_map(
        on_device,
        mesh=mesh,
        in_specs=(
            P("wave", "lev", None, None),
            P(),
            P(),
            P(),
            P("wave", None, None),
            P(),
            P("wave"),
        ),
        out_specs=P("lev", "wave", None),
        check_vma=False,
    )
```

```python
import functools
import math

import jax
import jax.numpy as jnp
from jax import lax
from jax.experimental import pallas as pl
from jax.experimental.pallas import tpu as pltpu
from jax.sharding import PartitionSpec as P

LONS = 5136
LANES = 128
CHUNK = 1280
FIRST = 1024
TAILS = (5, 4, 3, 2, 1)
SHORT = 512
F32, BF16 = jnp.float32, jnp.bfloat16


def up(size, to):
    return -(-size // to) * to


def split(x):
    hi = x.astype(BF16)
    return hi, (x - hi.astype(F32)).astype(BF16)


def dot(a, b, contract):
    return lax.dot_general(a, b, (contract, ((), ())), preferred_element_type=F32)


def turn(m, i, p, inv_p):
    x = m * i
    r = x - jnp.floor(x * inv_p) * p
    r = jnp.where(r < 0.0, r + p, r)
    r = jnp.where(r >= p, r - p, r)
    quarter = jnp.floor(4.0 * r * inv_p + 0.5)
    v = (4.0 * r - quarter * p) * ((math.pi / 2) * inv_p)
    s = v * v
    sin = v + v * s * (-1.0 / 6 + s * (1.0 / 120 + s * (-1.0 / 5040 + s * (1.0 / 362880))))
    cos = 1.0 + s * (-0.5 + s * (1.0 / 24 + s * (-1.0 / 720 + s * (1.0 / 40320))))
    odd = (quarter == 1.0) | (quarter == 3.0)
    a, b = jnp.where(odd, sin, cos), jnp.where(odd, cos, sin)
    return (
        jnp.where((quarter == 1.0) | (quarter == 2.0), -a, a),
        jnp.where((quarter == 2.0) | (quarter == 3.0), -b, b),
    )


def chunks(lons, first=0):
    starts = list(range(0, lons - CHUNK // 2, CHUNK))
    if first:
        starts.insert(1, first)
    return list(zip(starts, starts[1:] + [lons]))


def builds_early():
    return lax.axis_index("wave") < lax.axis_size("wave") // 4


def fetch(pairs, sems, first):
    copies = [pltpu.make_async_copy(a, b, sems.at[first + i]) for i, (a, b) in enumerate(pairs)]
    for copy in copies:
        copy.start()
    for copy in copies:
        copy.wait()


def build_table(ids_ref, pts_ref, table_ref):
    rows_here, lons = table_ref.shape[0], table_ref.shape[3]
    waves = table_ref.shape[2] // 2
    widest = up(max(end - start for start, end in chunks(lons)), LANES)
    row = lax.broadcasted_iota(jnp.int32, (waves, 1), 0)
    m = jnp.zeros((waves, 1), F32)
    for w in range(waves):
        m = jnp.where(row == w, ids_ref[w].astype(F32), m)
    lane = lax.broadcasted_iota(jnp.int32, (1, widest), 1).astype(F32)
    for j in range(rows_here):
        p = pts_ref[j].astype(F32)
        inv_p = 1.0 / jnp.full((1, 1), p, F32)
        weight = jnp.where(2.0 * m < p, jnp.where(m == 0.0, 1.0, 2.0), 0.0)
        cb, sb = turn(m, lane, p, inv_p)
        for start, end in chunks(lons):
            size = end - start
            ca, sa = turn(m, float(start), p, inv_p)
            ca, sa = ca * weight, sa * weight
            inside = lane < p - float(start)
            cos = jnp.where(inside, ca * cb - sa * sb, 0.0)
            sin = jnp.where(inside, -(sa * cb) - ca * sb, 0.0)
            hi, lo = split(jnp.concatenate([cos, sin], 0))
            table_ref[j, 0, :, start:end] = hi[:, :size]
            table_ref[j, 1, :, start:end] = lo[:, :size]


def send_kernel(
    lev_devices, waves,
    ids_hbm, to_hbm, depth_hbm, leg_hbm, from_hbm, spec_hbm, pts_hbm,
    out_ref, table_ref, limit_ref, grid_hbm,
    ids_ref, to_ref, depth_ref, leg_ref, from_ref, spec_ref, cols_ref, tile_ref, back_ref, pts_ref, zero_ref, sems,
):
    copies = [
        pltpu.make_async_copy(source, target, sems.at[i])
        for i, (source, target) in enumerate(
            (
                (depth_hbm, depth_ref),
                (to_hbm, to_ref),
                (leg_hbm, leg_ref),
                (ids_hbm, ids_ref),
                (spec_hbm, spec_ref),
                (from_hbm, from_ref),
            )
        )
    ]
    for copy in copies:
        copy.start()
    levels = to_ref.shape[0]
    here = levels // lev_devices
    orders = leg_ref.shape[2]
    rows_here = leg_ref.shape[1] // waves
    parts = 2 * rows_here
    modes_up, here_up = up(levels, 16), up(here, 16)
    lev, wave = lax.axis_index("lev"), lax.axis_index("wave")
    cols_ref[...] = jnp.zeros_like(cols_ref)
    back_ref[...] = jnp.zeros_like(back_ref)
    tile_ref[...] = jnp.zeros_like(tile_ref)
    copies[0].wait()

    eye = lax.broadcasted_iota(jnp.int32, (levels, levels), 0) == lax.broadcasted_iota(
        jnp.int32, (levels, levels), 1
    )
    depth = jnp.sum(jnp.where(eye, depth_ref[...][None, :], 0.0), axis=1, keepdims=True)
    depth = jnp.concatenate([depth, jnp.zeros((modes_up - levels, 1), F32)], 0)
    copies[1].wait()
    for d in range(lev_devices):

        @pl.when(lev == d)
        def _():
            x = to_ref[:, d * here : (d + 1) * here]
            hi = x.astype(BF16).astype(F32)
            cols_ref[:levels, 0:here] = hi
            cols_ref[:levels, here_up : here_up + here] = hi
            cols_ref[:levels, 2 * here_up : 2 * here_up + here] = x - hi

    copies[2].wait()
    copies[3].wait()
    own = ids_ref[wave]

    early = builds_early()
    lons = table_ref.shape[3]
    clears = [
        pltpu.make_async_copy(
            zero_ref.at[:, :, : end - start], grid_hbm.at[:, :, start:end], sems.at[7 + i]
        )
        for i, (start, end) in enumerate(chunks(lons))
    ]

    @pl.when(early)
    def _():
        zero_ref[...] = jnp.zeros_like(zero_ref)
        for clear in clears:
            clear.start()
        fetch(((pts_hbm, pts_ref),), sems, 6)
        longest = pts_ref[0]
        for j in range(1, rows_here):
            longest = jnp.maximum(longest, pts_ref[j])
        limit_ref[...] = jnp.full(limit_ref.shape, longest, jnp.int32).astype(F32)
        build_table(ids_ref, pts_ref, table_ref)

    def solve(low):
        tiles = range(low // LANES, orders // LANES)
        n = low + lax.broadcasted_iota(jnp.int32, (1, orders - low), 1)
        nf = n.astype(F32)
        inverse = 1.0 / (1.0 + depth * (nf * (nf + 1.0) / float(orders * orders)))
        cols = cols_ref[...].astype(BF16)
        for t in tiles:
            tile_ref[2, t, : leg_ref.shape[1]] = leg_ref[0, :, t * LANES : (t + 1) * LANES]
            for j in range(rows_here):
                x = tile_ref[2, t, pl.ds(j, waves, stride=rows_here), :]
                for c in range(2):
                    tile_ref[c, t, pl.ds(j * 2 * waves + c, waves, stride=2), :] = x
        keep = n >= own
        leg = [
            split(jnp.where(keep, jnp.concatenate([tile_ref[c, t] for t in tiles], 1), 0.0))
            for c in range(2)
        ]
        leg_hi = jnp.concatenate([leg[0][0], leg[1][0]], 1)
        leg_lo = jnp.concatenate([leg[0][1], leg[1][1]], 1)
        copies[4].wait()
        modes = []
        for c in range(2):
            zero = jnp.zeros((here_up - here, orders - low), F32)
            hi, lo = split(jnp.concatenate([spec_ref[0, :, c, low:], zero], 0))
            x = dot(cols, jnp.concatenate([hi, lo, hi], 0), ((1,), (0,)))
            modes.append(split(x * inverse))
        copies[5].wait()
        back = from_ref[...].T
        for d in range(lev_devices):
            back_ref[:levels, d * LANES : d * LANES + here] = back[:, d * here : (d + 1) * here]
        back_hi, back_lo = split(back_ref[...])
        hi = jnp.concatenate([modes[0][0], modes[1][0]], 1)
        lo = jnp.concatenate([modes[0][1], modes[1][1]], 1)
        width = parts * waves
        if orders - low <= SHORT:
            x = dot(
                jnp.concatenate([leg_hi, leg_lo, leg_hi], 1),
                jnp.concatenate([hi, hi, lo], 1),
                ((1,), (1,)),
            )
            hi, lo = split(x)
            x = dot(jnp.concatenate([hi, lo], 0), back_hi, ((1,), (0,)))
            four = x[:width] + (x[width:] + dot(hi, back_lo, ((1,), (0,))))
        else:
            x = dot(hi, jnp.concatenate([leg_hi, leg_lo], 0), ((1,), (1,)))
            y = dot(lo, leg_hi, ((1,), (1,)))
            hi, lo = split(x[:, :width] + (x[:, width:] + y))
            back = jnp.concatenate([back_hi, back_lo, back_hi], 0)
            four = dot(jnp.concatenate([hi, hi, lo], 0), back, ((0,), (0,)))
        rows = 2 * waves
        message = four[:rows]
        for j in range(1, rows_here):
            message = message + pltpu.roll(
                four[j * rows : (j + 1) * rows], j * (LANES // rows_here), 1
            )
        for d in range(lev_devices):
            out_ref[d * rows : (d + 1) * rows, :] = message[:, d * LANES : (d + 1) * LANES]

    lows = [0] + [orders - up(orders * tenths // 10, LANES) for tenths in TAILS]
    for low, above in zip(lows, lows[1:] + [orders]):
        pl.when((own >= low) & (own < above))(functools.partial(solve, low))

    @pl.when(early)
    def _():
        for clear in clears:
            clear.wait()


def grid_kernel(
    first_ref, limit_ref, got_ref, ids_hbm, pts_hbm, cleared_hbm,
    out_hbm,
    out_ref, table_ref, ids_ref, pts_ref, sems,
):
    here, rows_here, lons = out_ref.shape
    waves = table_ref.shape[2] // 2
    lev_devices = got_ref.shape[0] // (waves * 2)
    here_up = up(here, 8)
    early = builds_early()

    def left_sides():
        halves = []
        for c in range(2):
            total = None
            for d in range(lev_devices):
                x = got_ref[pl.ds((d * waves) * 2 + c, waves, stride=2), :]
                total = x if total is None else total + x
            halves.append(total)
        both = jnp.concatenate(halves, 0)
        left = []
        for j in range(rows_here):
            pitch = j * (LANES // rows_here)
            hi, lo = split(both[:, pitch : pitch + here_up])
            left.append(jnp.concatenate([hi, hi, lo], 0))
        return left

    def fill(ref, left, start, end):
        for j in range(rows_here):
            hi, lo = ref[j, 0, :, start:end], ref[j, 1, :, start:end]
            x = dot(left[j], jnp.concatenate([hi, lo, hi], 0), ((0,), (0,)))
            out_ref[:, j, start:end] = x[:here]

    def copy(i, start, end):
        return pltpu.make_async_copy(
            out_ref.at[:, :, start:end], out_hbm.at[:, :, start:end], sems.at[i]
        )

    @pl.when(early)
    def _():
        left = left_sides()
        limit = jnp.max(limit_ref[...]).astype(jnp.int32)
        parts_of = chunks(lons, FIRST)
        for i, (start, end) in enumerate(parts_of):

            def one():
                fill(first_ref, left, start, end)
                copy(i, start, end).start()

            one() if i == 0 else pl.when(start < limit)(one)
        for i, (start, end) in enumerate(parts_of):

            def done():
                copy(i, start, end).wait()

            done() if i == 0 else pl.when(start < limit)(done)

    @pl.when(jnp.logical_not(early))
    def _():
        fetch(((ids_hbm, ids_ref), (pts_hbm, pts_ref)), sems, 0)
        build_table(ids_ref, pts_ref, table_ref)
        left = left_sides()
        for i, (start, end) in enumerate(chunks(lons)):
            fill(table_ref, left, start, end)
            copy(i, start, end).start()
        for i, (start, end) in enumerate(chunks(lons)):
            copy(i, start, end).wait()


def on_device(spectral, to_modes, from_modes, mode_depths, legendre, wave_ids, lat_points):
    lev_devices, waves = lax.axis_size("lev"), lax.axis_size("wave")
    levels, orders = to_modes.shape[0], spectral.shape[3]
    here, rows_here = spectral.shape[1], lat_points.shape[0]
    assert up(here, 8) * rows_here <= LANES
    parts = 2 * rows_here
    vmem, hbm = pl.BlockSpec(memory_space=pltpu.VMEM), pl.BlockSpec(memory_space=pl.ANY)
    table = jax.ShapeDtypeStruct((rows_here, 2, 2 * waves, LONS), BF16)
    table_bytes = table.size * 2
    spectral, to_modes, from_modes, mode_depths, legendre, wave_ids, lat_points = (
        pltpu.with_memory_space_constraint(x, pltpu.HBM)
        for x in (spectral, to_modes, from_modes, mode_depths, legendre, wave_ids, lat_points)
    )
    widest = max(end - start for start, end in chunks(LONS))
    ids = [pltpu.SMEM(wave_ids.shape, jnp.int32), pltpu.SMEM(lat_points.shape, jnp.int32)]
    held = (to_modes, mode_depths, legendre, from_modes, spectral)
    grid = jax.ShapeDtypeStruct((here, rows_here, LONS), F32)
    blocks, first, limit, cleared = pl.pallas_call(
        functools.partial(send_kernel, lev_devices, waves),
        out_shape=(
            jax.ShapeDtypeStruct((lev_devices * waves * 2, LANES), F32),
            table,
            jax.ShapeDtypeStruct((8, LANES), F32),
            grid,
        ),
        in_specs=[hbm] * 7,
        out_specs=(vmem, vmem, vmem, hbm),
        scratch_shapes=[ids[0]]
        + [pltpu.VMEM(x.shape, F32) for x in held]
        + [
            pltpu.VMEM((up(levels, 16), 3 * up(here, 16)), F32),
            pltpu.VMEM((3, orders // LANES, parts * waves, LANES), F32),
            pltpu.VMEM((up(levels, 16), lev_devices * LANES), F32),
            ids[1],
            pltpu.VMEM((here, rows_here, widest), F32),
            pltpu.SemaphoreType.DMA((7 + len(chunks(LONS)),)),
        ],
        compiler_params=pltpu.CompilerParams(
            vmem_limit_bytes=(8 << 20) + 12 * orders * parts * waves * 4 + 2 * table_bytes
        ),
        name="send",
    )(wave_ids, *held, lat_points)
    got = lax.all_to_all(
        blocks.reshape(lev_devices * waves, 2, LANES), ("lev", "wave"), 0, 0, tiled=True
    ).reshape(blocks.shape)
    return pl.pallas_call(
        grid_kernel,
        out_shape=grid,
        in_specs=[vmem, vmem, vmem, hbm, hbm, hbm],
        input_output_aliases={5: 0},
        out_specs=hbm,
        scratch_shapes=[
            pltpu.VMEM((here, rows_here, LONS), F32),
            pltpu.VMEM(table.shape, BF16),
            *ids,
            pltpu.SemaphoreType.DMA((len(chunks(LONS, FIRST)),)),
        ],
        compiler_params=pltpu.CompilerParams(vmem_limit_bytes=(8 << 20) + 3 * table_bytes),
        name="grid",
    )(first, limit, got, wave_ids, lat_points, cleared)


def solution(mesh):
    return jax.shard_map(
        on_device,
        mesh=mesh,
        in_specs=(
            P("wave", "lev", None, None),
            P(),
            P(),
            P(),
            P("wave", None, None),
            P(),
            P("wave"),
        ),
        out_specs=P("lev", "wave", None),
        check_vma=False,
    )
```

```python
import functools
import math

import jax
import jax.numpy as jnp
from jax import lax
from jax.experimental import pallas as pl
from jax.experimental.pallas import tpu as pltpu
from jax.sharding import PartitionSpec as P

LONS = 5136
LANES = 128
CHUNK = 1280
FIRST = 1024
HEAD = 2
TAILS = (5, 4, 3, 2, 1)
SHORT = 512
F32, BF16 = jnp.float32, jnp.bfloat16


def up(size, to):
    return -(-size // to) * to


def split(x):
    hi = x.astype(BF16)
    return hi, (x - hi.astype(F32)).astype(BF16)


def dot(a, b, contract):
    return lax.dot_general(a, b, (contract, ((), ())), preferred_element_type=F32)


def turn(m, i, p, inv_p):
    x = m * i
    r = x - jnp.floor(x * inv_p) * p
    r = jnp.where(r < 0.0, r + p, r)
    r = jnp.where(r >= p, r - p, r)
    quarter = jnp.floor(4.0 * r * inv_p + 0.5)
    v = (4.0 * r - quarter * p) * ((math.pi / 2) * inv_p)
    s = v * v
    sin = v + v * s * (-1.0 / 6 + s * (1.0 / 120 + s * (-1.0 / 5040 + s * (1.0 / 362880))))
    cos = 1.0 + s * (-0.5 + s * (1.0 / 24 + s * (-1.0 / 720 + s * (1.0 / 40320))))
    odd = (quarter == 1.0) | (quarter == 3.0)
    a, b = jnp.where(odd, sin, cos), jnp.where(odd, cos, sin)
    return (
        jnp.where((quarter == 1.0) | (quarter == 2.0), -a, a),
        jnp.where((quarter == 2.0) | (quarter == 3.0), -b, b),
    )


def chunks(lons, first=0):
    starts = list(range(0, lons - CHUNK // 2, CHUNK))
    if first:
        starts.insert(1, first)
    return list(zip(starts, starts[1:] + [lons]))


def builds_early():
    return lax.axis_index("wave") < lax.axis_size("wave") // 4


def fetch(pairs, sems, first):
    copies = [pltpu.make_async_copy(a, b, sems.at[first + i]) for i, (a, b) in enumerate(pairs)]
    for copy in copies:
        copy.start()
    for copy in copies:
        copy.wait()


def build_table(ids_ref, pts_ref, table_ref):
    rows_here, lons = table_ref.shape[0], table_ref.shape[3]
    waves = table_ref.shape[2] // 2
    widest = up(max(end - start for start, end in chunks(lons)), LANES)
    row = lax.broadcasted_iota(jnp.int32, (waves, 1), 0)
    m = jnp.zeros((waves, 1), F32)
    for w in range(waves):
        m = jnp.where(row == w, ids_ref[w].astype(F32), m)
    lane = lax.broadcasted_iota(jnp.int32, (1, widest), 1).astype(F32)
    for j in range(rows_here):
        p = pts_ref[j].astype(F32)
        inv_p = 1.0 / jnp.full((1, 1), p, F32)
        weight = jnp.where(2.0 * m < p, jnp.where(m == 0.0, 1.0, 2.0), 0.0)
        cb, sb = turn(m, lane, p, inv_p)
        for start, end in chunks(lons):
            size = end - start
            ca, sa = turn(m, float(start), p, inv_p)
            ca, sa = ca * weight, sa * weight
            inside = lane < p - float(start)
            cos = jnp.where(inside, ca * cb - sa * sb, 0.0)
            sin = jnp.where(inside, -(sa * cb) - ca * sb, 0.0)
            hi, lo = split(jnp.concatenate([cos, sin], 0))
            table_ref[j, 0, :, start:end] = hi[:, :size]
            table_ref[j, 1, :, start:end] = lo[:, :size]


def send_kernel(
    lev_devices, waves,
    ids_hbm, to_hbm, depth_hbm, leg_hbm, from_hbm, spec_hbm, pts_hbm,
    out_ref, table_ref, limit_ref, grid_hbm,
    ids_ref, to_ref, depth_ref, leg_ref, from_ref, spec_ref, cols_ref, tile_ref, back_ref, pts_ref, zero_ref, sems,
):
    copies = [
        pltpu.make_async_copy(source, target, sems.at[i])
        for i, (source, target) in enumerate(
            (
                (depth_hbm, depth_ref),
                (to_hbm, to_ref),
                (leg_hbm, leg_ref),
                (ids_hbm, ids_ref),
                (spec_hbm, spec_ref),
                (from_hbm, from_ref),
            )
        )
    ]
    for copy in copies:
        copy.start()
    levels = to_ref.shape[0]
    here = levels // lev_devices
    orders = leg_ref.shape[2]
    rows_here = leg_ref.shape[1] // waves
    parts = 2 * rows_here
    modes_up, here_up = up(levels, 16), up(here, 16)
    lev, wave = lax.axis_index("lev"), lax.axis_index("wave")
    cols_ref[...] = jnp.zeros_like(cols_ref)
    back_ref[...] = jnp.zeros_like(back_ref)
    tile_ref[...] = jnp.zeros_like(tile_ref)
    copies[0].wait()

    eye = lax.broadcasted_iota(jnp.int32, (levels, levels), 0) == lax.broadcasted_iota(
        jnp.int32, (levels, levels), 1
    )
    depth = jnp.sum(jnp.where(eye, depth_ref[...][None, :], 0.0), axis=1, keepdims=True)
    depth = jnp.concatenate([depth, jnp.zeros((modes_up - levels, 1), F32)], 0)
    copies[1].wait()
    for d in range(lev_devices):

        @pl.when(lev == d)
        def _():
            x = to_ref[:, d * here : (d + 1) * here]
            hi = x.astype(BF16).astype(F32)
            cols_ref[:levels, 0:here] = hi
            cols_ref[:levels, here_up : here_up + here] = hi
            cols_ref[:levels, 2 * here_up : 2 * here_up + here] = x - hi

    copies[2].wait()
    copies[3].wait()
    own = ids_ref[wave]

    early = builds_early()
    lons = table_ref.shape[3]
    clears = [
        pltpu.make_async_copy(
            zero_ref.at[:, :, : end - start], grid_hbm.at[:, :, start:end], sems.at[7 + i]
        )
        for i, (start, end) in enumerate(chunks(lons))
    ]

    @pl.when(early)
    def _():
        zero_ref[...] = jnp.zeros_like(zero_ref)
        for clear in clears:
            clear.start()
        fetch(((pts_hbm, pts_ref),), sems, 6)
        longest = pts_ref[0]
        for j in range(1, rows_here):
            longest = jnp.maximum(longest, pts_ref[j])
        limit_ref[...] = jnp.full(limit_ref.shape, longest, jnp.int32).astype(F32)
        build_table(ids_ref, pts_ref, table_ref)

    def solve(low):
        tiles = range(low // LANES, orders // LANES)
        n = low + lax.broadcasted_iota(jnp.int32, (1, orders - low), 1)
        nf = n.astype(F32)
        inverse = 1.0 / (1.0 + depth * (nf * (nf + 1.0) / float(orders * orders)))
        cols = cols_ref[...].astype(BF16)
        for t in tiles:
            tile_ref[2, t, : leg_ref.shape[1]] = leg_ref[0, :, t * LANES : (t + 1) * LANES]
            for j in range(rows_here):
                x = tile_ref[2, t, pl.ds(j, waves, stride=rows_here), :]
                for c in range(2):
                    tile_ref[c, t, pl.ds(c * rows_here + j, waves, stride=parts), :] = x
        keep = n >= own
        leg = [
            split(jnp.where(keep, jnp.concatenate([tile_ref[c, t] for t in tiles], 1), 0.0))
            for c in range(2)
        ]
        leg_hi = jnp.concatenate([leg[0][0], leg[1][0]], 1)
        leg_lo = jnp.concatenate([leg[0][1], leg[1][1]], 1)
        copies[4].wait()
        modes = []
        for c in range(2):
            zero = jnp.zeros((here_up - here, orders - low), F32)
            hi, lo = split(jnp.concatenate([spec_ref[0, :, c, low:], zero], 0))
            x = dot(cols, jnp.concatenate([hi, lo, hi], 0), ((1,), (0,)))
            modes.append(split(x * inverse))
        copies[5].wait()
        back = from_ref[...].T
        for d in range(lev_devices):
            back_ref[:levels, d * LANES : d * LANES + here] = back[:, d * here : (d + 1) * here]
        back_hi, back_lo = split(back_ref[...])
        hi = jnp.concatenate([modes[0][0], modes[1][0]], 1)
        lo = jnp.concatenate([modes[0][1], modes[1][1]], 1)
        width = parts * waves
        if orders - low <= SHORT:
            x = dot(
                jnp.concatenate([leg_hi, leg_lo, leg_hi], 1),
                jnp.concatenate([hi, hi, lo], 1),
                ((1,), (1,)),
            )
            hi, lo = split(x)
            x = dot(jnp.concatenate([hi, lo], 0), back_hi, ((1,), (0,)))
            four = x[:width] + (x[width:] + dot(hi, back_lo, ((1,), (0,))))
        else:
            x = dot(hi, jnp.concatenate([leg_hi, leg_lo], 0), ((1,), (1,)))
            y = dot(lo, leg_hi, ((1,), (1,)))
            hi, lo = split(x[:, :width] + (x[:, width:] + y))
            back = jnp.concatenate([back_hi, back_lo, back_hi], 0)
            four = dot(jnp.concatenate([hi, hi, lo], 0), back, ((0,), (0,)))
        for d in range(lev_devices):
            out_ref[d * width : (d + 1) * width, :] = four[:, d * LANES : (d + 1) * LANES]

    lows = [0] + [orders - up(orders * tenths // 10, LANES) for tenths in TAILS]
    for low, above in zip(lows, lows[1:] + [orders]):
        pl.when((own >= low) & (own < above))(functools.partial(solve, low))

    @pl.when(early)
    def _():
        for clear in clears:
            clear.wait()


def grid_kernel(
    first_ref, limit_ref, got_ref, ids_hbm, pts_hbm, cleared_hbm,
    out_hbm,
    out_ref, table_ref, ids_ref, pts_ref, sems,
):
    here, rows_here, lons = out_ref.shape
    parts = 2 * rows_here
    waves = table_ref.shape[2] // 2
    lev_devices = got_ref.shape[0] // (waves * parts)
    here_up = up(here, 8)
    early = builds_early()

    def left_sides():
        left = []
        for j in range(rows_here):
            halves = []
            for c in range(2):
                total = None
                for d in range(lev_devices):
                    x = got_ref[pl.ds(d * waves * parts + c * rows_here + j, waves, stride=parts), :]
                    total = x if total is None else total + x
                halves.append(total)
            hi, lo = split(jnp.concatenate(halves, 0)[:, :here_up])
            left.append(jnp.concatenate([hi, hi, lo], 0))
        return left

    def fill(ref, left, start, end):
        for j in range(rows_here):
            hi, lo = ref[j, 0, :, start:end], ref[j, 1, :, start:end]
            x = dot(left[j], jnp.concatenate([hi, lo, hi], 0), ((0,), (0,)))
            out_ref[:, j, start:end] = x[:here]

    def copy(i, start, end):
        return pltpu.make_async_copy(
            out_ref.at[:, :, start:end], out_hbm.at[:, :, start:end], sems.at[i]
        )

    @pl.when(early)
    def _():
        left = left_sides()
        pieces = chunks(lons, FIRST)
        first = pieces[0][1]
        cuts = [(i * first // HEAD, (i + 1) * first // HEAD) for i in range(HEAD)]
        for i, (start, end) in enumerate(cuts):
            fill(first_ref, left, start, end)
            copy(i, start, end).start()
        limit = jnp.max(limit_ref[...]).astype(jnp.int32)

        @pl.when(first < limit)
        def _():
            for i, (start, end) in enumerate(pieces[1:], HEAD):

                def one():
                    fill(first_ref, left, start, end)
                    copy(i, start, end).start()

                pl.when(start < limit)(one)
            for i, (start, end) in enumerate(pieces[1:], HEAD):
                pl.when(start < limit)(copy(i, start, end).wait)

        for i, (start, end) in enumerate(cuts):
            copy(i, start, end).wait()

    @pl.when(jnp.logical_not(early))
    def _():
        fetch(((ids_hbm, ids_ref), (pts_hbm, pts_ref)), sems, 0)
        build_table(ids_ref, pts_ref, table_ref)
        left = left_sides()
        for i, (start, end) in enumerate(chunks(lons)):
            fill(table_ref, left, start, end)
            copy(i, start, end).start()
        for i, (start, end) in enumerate(chunks(lons)):
            copy(i, start, end).wait()


def on_device(spectral, to_modes, from_modes, mode_depths, legendre, wave_ids, lat_points):
    lev_devices, waves = lax.axis_size("lev"), lax.axis_size("wave")
    levels, orders = to_modes.shape[0], spectral.shape[3]
    here, rows_here = spectral.shape[1], lat_points.shape[0]
    parts = 2 * rows_here
    vmem, hbm = pl.BlockSpec(memory_space=pltpu.VMEM), pl.BlockSpec(memory_space=pl.ANY)
    table = jax.ShapeDtypeStruct((rows_here, 2, 2 * waves, LONS), BF16)
    table_bytes = table.size * 2
    spectral, to_modes, from_modes, mode_depths, legendre, wave_ids, lat_points = (
        pltpu.with_memory_space_constraint(x, pltpu.HBM)
        for x in (spectral, to_modes, from_modes, mode_depths, legendre, wave_ids, lat_points)
    )
    widest = max(end - start for start, end in chunks(LONS))
    ids = [pltpu.SMEM(wave_ids.shape, jnp.int32), pltpu.SMEM(lat_points.shape, jnp.int32)]
    held = (to_modes, mode_depths, legendre, from_modes, spectral)
    grid = jax.ShapeDtypeStruct((here, rows_here, LONS), F32)
    blocks, first, limit, cleared = pl.pallas_call(
        functools.partial(send_kernel, lev_devices, waves),
        out_shape=(
            jax.ShapeDtypeStruct((lev_devices * waves * parts, LANES), F32),
            table,
            jax.ShapeDtypeStruct((8, LANES), F32),
            grid,
        ),
        in_specs=[hbm] * 7,
        out_specs=(vmem, vmem, vmem, hbm),
        scratch_shapes=[ids[0]]
        + [pltpu.VMEM(x.shape, F32) for x in held]
        + [
            pltpu.VMEM((up(levels, 16), 3 * up(here, 16)), F32),
            pltpu.VMEM((3, orders // LANES, parts * waves, LANES), F32),
            pltpu.VMEM((up(levels, 16), lev_devices * LANES), F32),
            ids[1],
            pltpu.VMEM((here, rows_here, widest), F32),
            pltpu.SemaphoreType.DMA((7 + len(chunks(LONS)),)),
        ],
        compiler_params=pltpu.CompilerParams(
            vmem_limit_bytes=(8 << 20) + 12 * orders * parts * waves * 4 + 2 * table_bytes
        ),
        name="send",
    )(wave_ids, *held, lat_points)
    got = lax.all_to_all(
        blocks.reshape(lev_devices * waves, parts, LANES), ("lev", "wave"), 0, 0, tiled=True
    ).reshape(blocks.shape)
    return pl.pallas_call(
        grid_kernel,
        out_shape=grid,
        in_specs=[vmem, vmem, vmem, hbm, hbm, hbm],
        input_output_aliases={5: 0},
        out_specs=hbm,
        scratch_shapes=[
            pltpu.VMEM((here, rows_here, LONS), F32),
            pltpu.VMEM(table.shape, BF16),
            *ids,
            pltpu.SemaphoreType.DMA((len(chunks(LONS, FIRST)) + HEAD,)),
        ],
        compiler_params=pltpu.CompilerParams(vmem_limit_bytes=(8 << 20) + 3 * table_bytes),
        name="grid",
    )(first, limit, got, wave_ids, lat_points, cleared)


def solution(mesh):
    return jax.shard_map(
        on_device,
        mesh=mesh,
        in_specs=(
            P("wave", "lev", None, None),
            P(),
            P(),
            P(),
            P("wave", None, None),
            P(),
            P("wave"),
        ),
        out_specs=P("lev", "wave", None),
        check_vma=False,
    )
```
